32 devices in a mesh: dom: 8 (over z, x), feat: 4 (over y, core).
Axes of the slice: x: 2, y: 2, z: 4, core: 2. Of those that a mesh axis runs over, the one named last changes fastest.
Arguments:
- features: bfloat16 [8192, 1024], P('dom', 'feat'), may hold values from -6 to 6
- adjacency: bfloat16 [64, 16, 128, 128], P('dom'), may hold values from -0.125 to 0.125
- tile_src: int32 [64, 16], replicated, may hold values from 0 to 63, as said below
- mig_slot: int32 [8, 2], replicated, may hold values from 0 to 7, as said below
- weight_one: bfloat16 [1024, 1024], replicated, may hold values from -0.1875 to 0.1875
- weight_two: bfloat16 [1024, 1024], replicated, may hold values from -0.1875 to 0.1875
Outputs:
- mixed: bfloat16 [8192, 1024], P('dom', 'feat')
The draws below stay inside these ranges and needn't reach their ends.
Inputs may be any that keep to these rules, and one draw needn't show every extreme that they name: `tile_src`: the tiles of the row blocks that one partition holds name at most 2 distinct blocks held by any one other partition, both in the starting placement and in the placement after the move; in the starting placement they name exactly 2 blocks of every other partition, one of which leaves that partition in the move. `mig_slot`: each row holds 2 distinct slots.
All inputs are finite; a program needn't handle non-finite values.
Results may differ from the reference program's by a relative error of at most 0.0064.
Values may be sent and summed in bfloat16 or wider, within the bound.
No kernel may reach another device: no remote copies, remote signals or barrier semaphores. Data moves between devices by JAX's collectives and lax.ppermute only.
A program may use at most 128 MiB of HBM per device.

```python
import jax
import jax.numpy as jnp
from jax import lax

F = 1024
B = 128
R = 8
TPB = 16
MIG = 2
NB = 64
NODES = 8192
N_DOM = 8


def pick_list(key, values, usable, filler, wanted, salt):
    block_pool = jnp.concatenate([values, filler], axis=1)
    pool_width = block_pool.shape[1]
    rank_class = jnp.concatenate([jnp.where(usable, 0, 2), jnp.zeros_like(filler) + 1], axis=1).astype(jnp.int32)
    ranking = jnp.argsort(rank_class * pool_width + jnp.arange(pool_width, dtype=jnp.int32)[None, :], axis=1, stable=True)
    chosen = jnp.take_along_axis(block_pool, ranking[:, :wanted], axis=1)
    shuffle_scores = jax.random.randint(jax.random.fold_in(key, salt), (N_DOM, wanted), 0, 1048576) * wanted + jnp.arange(wanted, dtype=jnp.int32)[None, :]
    shuffle = jnp.argsort(shuffle_scores, axis=1, stable=True)
    return jnp.take_along_axis(chosen, shuffle, axis=1)


def layout_draw(key):
    domain_ids = jnp.arange(N_DOM, dtype=jnp.int32)
    slot_scores = jax.random.randint(jax.random.fold_in(key, 11), (N_DOM, R), 0, 1048576) * R + jnp.arange(R, dtype=jnp.int32)[None, :]
    slot_order = jnp.argsort(slot_scores, axis=1, stable=True).astype(jnp.int32)
    mig_slots = slot_order[:, :MIG]
    leave_total = MIG * TPB
    stay_total = (R - MIG) * TPB
    group_count = min(leave_total, N_DOM)
    group_scores = jax.random.randint(jax.random.fold_in(key, 12), (N_DOM,), 0, 1048576) * N_DOM + domain_ids
    group_rank = jnp.argsort(jnp.argsort(group_scores, stable=True), stable=True)
    in_group = group_rank < group_count
    move_pick = jax.random.randint(jax.random.fold_in(key, 13), (N_DOM, N_DOM), 0, MIG)
    stay_pick = jax.random.randint(jax.random.fold_in(key, 14), (N_DOM, N_DOM), 0, R - MIG)
    peer_index = jnp.broadcast_to(domain_ids[None, :], (N_DOM, N_DOM))
    moving_named = peer_index * R + slot_order[peer_index, move_pick]
    staying_named = peer_index * R + slot_order[peer_index, MIG + stay_pick]
    not_self = domain_ids[:, None] != domain_ids[None, :]
    leave_usable = not_self & in_group[None, :]
    stay_usable = not_self & jnp.logical_not(in_group)[None, :]
    own_move = domain_ids[:, None] * R + jnp.take_along_axis(slot_order, jax.random.randint(jax.random.fold_in(key, 15), (N_DOM, leave_total), 0, MIG), axis=1)
    own_stay = domain_ids[:, None] * R + jnp.take_along_axis(slot_order, MIG + jax.random.randint(jax.random.fold_in(key, 16), (N_DOM, stay_total), 0, R - MIG), axis=1)
    leaving_list = pick_list(key, staying_named, leave_usable, own_move, leave_total, 17)
    staying_list = pick_list(key, jnp.concatenate([moving_named, staying_named], axis=1), jnp.concatenate([not_self, stay_usable], axis=1), own_stay, stay_total, 18)
    by_order = jnp.concatenate([leaving_list, staying_list], axis=1).reshape(N_DOM, R, TPB)
    inverse = jnp.argsort(slot_order, axis=1, stable=True)
    listing = jnp.take_along_axis(by_order, inverse[:, :, None], axis=1)
    return (mig_slots.astype(jnp.int32), listing.reshape(N_DOM * R, TPB).astype(jnp.int32))


def draw_tile_src(key, part):
    return layout_draw(key)[1]


def draw_mig_slot(key, part):
    return layout_draw(key)[0]


def levels(rng, dims, pieces, least, high):
    def one(axis_at, parts):
        heights = jax.random.uniform(jax.random.fold_in(jax.random.fold_in(rng, 6), axis_at), (parts,), jnp.float32, least / len(pieces), high / len(pieces))
        return jnp.repeat(jnp.exp(heights), dims[axis_at] // parts).reshape((-1,) + (1,) * (len(dims) - axis_at - 1))

    factor_of = one(*pieces[0])
    for cut in pieces[1:]:
        factor_of = factor_of * one(*cut)
    return factor_of


def noise(stream_key, extent, width, most, cuts=(), held_as=jnp.bfloat16):
    values = width * jax.random.normal(stream_key, extent, jnp.float32)
    if cuts:
        values = values * levels(stream_key, extent, cuts, -0.22, 0.18)
    return jnp.clip(values, -most, most).astype(held_as)


def setup_inputs(seed: int = 0) -> dict:
    streams_of = jax.random.split(jax.random.key(seed), 7)
    features = noise(streams_of[0], (NODES, F), 1.0, 6.0, ((0, 8), (1, 4)))
    adjacency = noise(streams_of[1], (NB, TPB, B, B), (TPB * B) ** -0.5, 0.125, ((0, 8),))
    tile_src = draw_tile_src(jax.random.fold_in(streams_of[6], 71), 0)
    mig_slot = draw_mig_slot(jax.random.fold_in(streams_of[6], 71), 0)
    weight_one = noise(streams_of[4], (F, F), F ** -0.5, 0.1875)
    weight_two = noise(streams_of[5], (F, F), F ** -0.5, 0.1875)
    return {"features": features, "adjacency": adjacency, "tile_src": tile_src, "mig_slot": mig_slot, "weight_one": weight_one, "weight_two": weight_two}


def apply_layer(inputs, adjacency, tile_src, weight):
    def per_domain(domain):
        source_ids = lax.dynamic_slice_in_dim(tile_src, domain * R, R, 0)
        tiles_here = lax.dynamic_slice_in_dim(adjacency, domain * R, R, 0)
        gathered = inputs[source_ids]
        summed = jnp.einsum('rtij,rtjf->rif', tiles_here.astype(jnp.float32), gathered.astype(jnp.float32))
        agg_rows = summed.astype(jnp.bfloat16).reshape(R * B, F)
        return jnp.dot(agg_rows, weight, preferred_element_type=jnp.float32)
    result = lax.map(per_domain, jnp.arange(N_DOM, dtype=jnp.int32))
    return result.reshape(N_DOM * R, B, F)


def reference(features, adjacency, tile_src, mig_slot, weight_one, weight_two):
    blocks_in = features.reshape(N_DOM * R, B, F)
    hidden = jax.nn.relu(apply_layer(blocks_in, adjacency, tile_src, weight_one)).astype(jnp.bfloat16)
    result = apply_layer(hidden, adjacency, tile_src, weight_two)
    domain_ids = jnp.arange(N_DOM, dtype=jnp.int32)
    block_ids = (domain_ids[:, None] * R + jnp.arange(R, dtype=jnp.int32)[None, :]).astype(jnp.int32)
    previous = (((domain_ids - 1) % N_DOM) * R)[:, None] + jnp.roll(mig_slot, 1, axis=0)
    new_ids = block_ids.at[domain_ids[:, None], mig_slot].set(previous.astype(jnp.int32))
    placed = result[new_ids.reshape(-1)]
    return placed.reshape(N_DOM * R * B, F).astype(jnp.bfloat16)
```

```python
import functools

import jax
import jax.numpy as jnp
from jax import lax
from jax.experimental import pallas as pl
from jax.experimental.pallas import tpu as pltpu
from jax.sharding import PartitionSpec as P


BF16 = jnp.bfloat16
F32 = jnp.float32
I32 = jnp.int32
VMEM = pl.BlockSpec(memory_space=pltpu.VMEM)
SMEM = pl.BlockSpec(memory_space=pltpu.SMEM)
ANY = pl.BlockSpec(memory_space=pl.ANY)


def swap(value, axis, flip):
    return lax.ppermute(value, axis, [(i, i ^ flip) for i in range(lax.axis_size(axis))])


def block(shape, dtype=BF16):
    return jax.ShapeDtypeStruct(shape, dtype)


def write_sends(domains, slots_ref, read, pair_ref, near_refs, far_refs):
    half = domains // 2
    pair_ref[0] = read(slots_ref[0])
    pair_ref[1] = read(slots_ref[1])
    for k in range(half, domains):
        far_refs[k - half][0] = read(slots_ref[2 * k + 2])
    for k in range(1, half):
        near_refs[k - 1][0] = read(slots_ref[2 * k + 1])
        near_refs[k - 1][1] = read(slots_ref[2 * k + 2])


def first_kernel(domains, rows, tiles_ref, mig_ref, x_ref, table_ref, slots_ref, which_ref, *sends):
    half = domains // 2
    me = lax.axis_index("dom")
    mine0, mine1 = mig_ref[me, 0], mig_ref[me, 1]
    slots_ref[0] = mine0
    slots_ref[1] = mine1
    opposite = me ^ half
    opposite_last = opposite * rows + mig_ref[opposite, 1]

    def requests(k):
        peer = me ^ k
        named = tiles_ref[pl.ds(pl.multiple_of(peer * rows, rows), rows), :]
        slot = named - me * rows
        inside = (slot >= 0) & (slot < rows)
        leaves = (slot == mine0) | (slot == mine1)
        staying = jnp.max(jnp.where(inside & jnp.logical_not(leaves), slot, 0))
        last = jnp.max(jnp.where(slot == mine1, 1, 0))
        slots_ref[2 * k + 1] = jnp.where(last == 1, mine1, mine0)
        slots_ref[2 * k + 2] = staying
        which_ref[k] = jnp.max(jnp.where(named == opposite_last, 1, 0))

    if domains <= 16:
        for k in range(1, domains):
            requests(k)
    else:
        pl.loop(1, domains)(requests)
    write_sends(domains, slots_ref, lambda s: x_ref[s], sends[0], sends[1:half], sends[half:])

    own = tiles_ref[pl.ds(pl.multiple_of(me * rows, rows), rows), :]
    holder = own // rows
    slot = own - holder * rows
    flip = holder ^ me

    def mark(q, carry):
        first, last = carry
        here = holder == q
        first = first | (here & (slot == mig_ref[q, 0])).astype(I32)
        last = last | (here & (slot == mig_ref[q, 1])).astype(I32)
        return first, last

    zeros = jnp.zeros_like(own)
    first, last = lax.fori_loop(0, domains, mark, (zeros, zeros))
    leaves = first | last
    place = rows + 2 * flip + 1 - leaves
    place = jnp.where((flip == half) & (leaves == 1), rows + last, place)
    table_ref[...] = jnp.where(flip == 0, slot, place)


def relay_kernel(half, which_ref, pair_ref, *outs):
    for k in range(1, half):
        outs[k - 1][0] = pair_ref[which_ref[k]]


def fill_pool(domains, chunks, pair_ref, near_refs, far_refs, relay_refs, pool_ref):
    half = domains // 2
    per = chunks[0].shape[0]
    rows = per * len(chunks)
    if len(chunks) == 1:
        pool_ref[0:rows] = chunks[0][...]
    else:
        feat = lax.axis_index("feat")
        for j, chunk in enumerate(chunks):
            for i in range(per):
                pool_ref[(feat ^ j) * per + i] = chunk[i]
    pool_ref[rows : rows + 2] = pair_ref[...]
    for k in range(1, half):
        pool_ref[rows + 2 * k : rows + 2 * k + 2] = near_refs[k - 1][...]
    for k in range(half, domains):
        pool_ref[rows + 2 * k + 1] = far_refs[k - half][0]
        if k > half:
            pool_ref[rows + 2 * k] = relay_refs[k - half - 1][0]


def sum_row(r, table_ref, adjacency_ref, pool_ref):
    tiles = adjacency_ref.shape[1]
    total = None
    for t in range(0, tiles, 2):
        left = jnp.concatenate([adjacency_ref[r, t], adjacency_ref[r, t + 1]], axis=1)
        right = jnp.concatenate(
            [pool_ref[table_ref[r, t]], pool_ref[table_ref[r, t + 1]]], axis=0
        )
        part = jnp.dot(left, right, preferred_element_type=F32)
        total = part if total is None else total + part
    return total.astype(BF16)


def split_refs(domains, n_chunks, refs):
    half = domains // 2
    chunks, refs = refs[:n_chunks], refs[n_chunks:]
    pair, refs = refs[0], refs[1:]
    near, refs = refs[: half - 1], refs[half - 1 :]
    far, refs = refs[:half], refs[half:]
    relay, rest = refs[: half - 1], refs[half - 1 :]
    return chunks, pair, near, far, relay, rest


def aggregate_first_kernel(domains, feats, table_ref, adjacency_ref, *refs):
    chunks, pair, near, far, relay, rest = split_refs(domains, 1, refs)
    outs, pool_ref = rest[:-1], rest[-1]
    fill_pool(domains, chunks, pair, near, far, relay, pool_ref)
    feat = lax.axis_index("feat")
    per = adjacency_ref.shape[0] // feats
    for j in range(feats):

        @pl.loop(0, per)
        def _(i, j=j):
            outs[j][i] = sum_row((feat ^ j) * per + i, table_ref, adjacency_ref, pool_ref)


def aggregate_leaving_kernel(domains, feats, table_ref, slots_ref, adjacency_ref, *refs):
    chunks, pair, near, far, relay, rest = split_refs(domains, feats, refs)
    out_ref, pool_ref = rest
    fill_pool(domains, chunks, pair, near, far, relay, pool_ref)

    @pl.loop(0, out_ref.shape[0])
    def _(i):
        out_ref[i] = sum_row(slots_ref[i], table_ref, adjacency_ref, pool_ref)


def aggregate_staying_kernel(domains, feats, table_ref, slots_ref, adjacency_ref, *refs):
    chunks, pair, near, far, relay, rest = split_refs(domains, feats, refs)
    out_ref, pool_ref = rest
    fill_pool(domains, chunks, pair, near, far, relay, pool_ref)

    @pl.loop(0, out_ref.shape[0])
    def _(r):
        @pl.when((r != slots_ref[0]) & (r != slots_ref[1]))
        def _():
            out_ref[r] = sum_row(r, table_ref, adjacency_ref, pool_ref)


def dense_kernel(feats, weight_one_ref, weight_two_ref, *refs):
    parts, outs, hidden_ref = refs[:feats], refs[feats : 2 * feats], refs[2 * feats]
    feat = lax.axis_index("feat")
    rows = parts[0].shape[0]
    width = parts[0].shape[1]
    columns = weight_one_ref.shape[1]
    for c in range(0, columns, width):
        total = None
        for j in range(feats):
            start = pl.multiple_of((feat ^ j) * width, width)
            part = jnp.dot(
                parts[j][...],
                weight_one_ref[pl.ds(start, width), c : c + width],
                preferred_element_type=F32,
            )
            total = part if total is None else total + part
        hidden_ref[:, c : c + width] = jnp.maximum(total, 0.0).astype(BF16)
    for j in range(feats):
        start = pl.multiple_of((feat ^ j) * width, width)
        outs[j][...] = jnp.dot(
            hidden_ref[...],
            weight_two_ref[:, pl.ds(start, width)],
            preferred_element_type=F32,
        ).astype(BF16)


def second_kernel(domains, feats, slots_ref, *refs):
    chunks, sends = refs[:feats], refs[feats:]
    half = domains // 2
    own_ref = sends[-1]
    sends = sends[:-1]
    per = chunks[0].shape[0]
    feat = lax.axis_index("feat")
    for j, chunk in enumerate(chunks):
        for i in range(per):
            own_ref[(feat ^ j) * per + i] = chunk[i]
    write_sends(domains, slots_ref, lambda s: own_ref[s], sends[0], sends[1:half], sends[half:])


def place_kernel(slots_ref, moved_ref, out_in_ref, out_ref, sems):
    del out_in_ref
    copies = [
        pltpu.make_async_copy(moved_ref.at[i], out_ref.at[slots_ref[i]], sems.at[i])
        for i in range(moved_ref.shape[0])
    ]
    for copy in copies:
        copy.start()
    for copy in copies:
        copy.wait()


def call(kernel, name, out_shape, in_specs, out_specs, scratch=(), flops=0, moved=0, **kwargs):
    return pl.pallas_call(
        kernel,
        name=name,
        out_shape=out_shape,
        in_specs=in_specs,
        out_specs=out_specs,
        scratch_shapes=list(scratch),
        cost_estimate=pl.CostEstimate(flops=flops, bytes_accessed=moved, transcendentals=0),
        **kwargs,
    )


def send_shapes(domains, size, width):
    half = domains // 2
    return (
        [block((2, size, width))]
        + [block((2, size, width))] * (half - 1)
        + [block((1, size, width))] * half
    )


def exchange(domains, sends, which, size, width, name):
    half = domains // 2
    pair = swap(sends[0], "dom", half)
    far = [swap(sends[k], "dom", k) for k in range(half, domains)]
    near = [swap(sends[k], "dom", k) for k in range(1, half)]
    relayed = call(
        functools.partial(relay_kernel, half),
        name,
        [block((1, size, width))] * (half - 1),
        [SMEM, VMEM],
        [VMEM] * (half - 1),
        moved=4 * size * width * (half - 1),
    )(which, pair)
    relay = [swap(relayed[k - 1], "dom", k) for k in range(1, half)]
    return [pair, *near, *far, *relay]


def on_device(features, adjacency, tile_src, mig_slot, weight_one, weight_two):
    domains = lax.axis_size("dom")
    feats = lax.axis_size("feat")
    half = domains // 2
    rows, tiles, size, _ = adjacency.shape
    width = features.shape[1]
    per = rows // feats
    blocks = features.reshape(rows, size, width)
    n_sends = domains
    pool = pltpu.VMEM((rows + 2 * domains, size, width), BF16)
    work = 2 * rows * tiles * size * size * width
    read = adjacency.size * 2

    table, slots, which, *sends = call(
        functools.partial(first_kernel, domains, rows),
        "first_sends",
        [block((rows, tiles), I32), block((2 * domains + 1,), I32), block((domains,), I32)]
        + send_shapes(domains, size, width),
        [VMEM, SMEM, VMEM],
        [VMEM, SMEM, SMEM] + [VMEM] * n_sends,
        moved=4 * size * width * 2 * domains,
    )(tile_src, mig_slot, blocks)
    arrived = exchange(domains, sends, which, size, width, "first_relay")

    parts = call(
        functools.partial(aggregate_first_kernel, domains, feats),
        "first_sum",
        [block((per, size, width))] * feats,
        [SMEM] + [VMEM] * (2 + len(arrived)),
        [VMEM] * feats,
        [pool],
        flops=work,
        moved=read,
    )(table, adjacency, blocks, *arrived)
    parts = [p.reshape(per * size, width) for p in parts]
    parts = [parts[0]] + [swap(parts[j], "feat", j) for j in range(1, feats)]

    chunks = call(
        functools.partial(dense_kernel, feats),
        "dense",
        [block((per * size, width))] * feats,
        [VMEM] * (2 + feats),
        [VMEM] * feats,
        [pltpu.VMEM((per * size, weight_one.shape[1]), BF16)],
        flops=4 * per * size * weight_one.size,
        moved=weight_one.size * 4,
    )(weight_one, weight_two, *parts)
    chunks = [chunks[0]] + [swap(chunks[j], "feat", j) for j in range(1, feats)]
    chunks = [c.reshape(per, size, width) for c in chunks]

    sends = call(
        functools.partial(second_kernel, domains, feats),
        "second_sends",
        send_shapes(domains, size, width),
        [SMEM] + [VMEM] * feats,
        [VMEM] * n_sends,
        [pltpu.VMEM((rows, size, width), BF16)],
        moved=4 * size * width * 2 * domains,
    )(slots, *chunks)
    arrived = exchange(domains, sends, which, size, width, "second_relay")

    leaving = call(
        functools.partial(aggregate_leaving_kernel, domains, feats),
        "leaving_sum",
        block((2, size, width)),
        [SMEM, SMEM] + [VMEM] * (1 + feats + len(arrived)),
        VMEM,
        [pool],
        flops=work // 4,
        moved=read // 4,
    )(table, slots, adjacency, *chunks, *arrived)
    moved = lax.ppermute(leaving, "dom", [(i, (i + 1) % domains) for i in range(domains)])
    out = call(
        functools.partial(aggregate_staying_kernel, domains, feats),
        "staying_sum",
        block((rows, size, width)),
        [SMEM, SMEM] + [VMEM] * (1 + feats + len(arrived)),
        VMEM,
        [pool],
        flops=work * 3 // 4,
        moved=read * 3 // 4,
    )(table, slots, adjacency, *chunks, *arrived)
    out = call(
        place_kernel,
        "place",
        block((rows, size, width)),
        [SMEM, VMEM, ANY],
        ANY,
        [pltpu.SemaphoreType.DMA((2,))],
        moved=4 * size * width * 2,
        input_output_aliases={2: 0},
    )(slots, moved, out)
    return out.reshape(rows * size, width)


def solution(mesh):
    in_specs = (P("dom", "feat"), P("dom", None, None, None), P(), P(), P(), P())
    return jax.shard_map(
        on_device, mesh=mesh, in_specs=in_specs, out_specs=P("dom", "feat"), check_vma=False
    )
```

```python
import functools

import jax
import jax.numpy as jnp
from jax import lax
from jax.experimental import pallas as pl
from jax.experimental.pallas import tpu as pltpu
from jax.sharding import PartitionSpec as P


BF16 = jnp.bfloat16
F32 = jnp.float32
I32 = jnp.int32
VMEM = pl.BlockSpec(memory_space=pltpu.VMEM)
SMEM = pl.BlockSpec(memory_space=pltpu.SMEM)
ANY = pl.BlockSpec(memory_space=pl.ANY)
HBM = pl.BlockSpec(memory_space=pltpu.HBM)


def swap(value, axis, flip):
    return lax.ppermute(value, axis, [(i, i ^ flip) for i in range(lax.axis_size(axis))])


def block(shape, dtype=BF16):
    return pltpu.VMEM(shape, dtype)


def write_sends(domains, slots_ref, read, pair_ref, near_refs, far_refs):
    half = domains // 2
    pair_ref[0] = read(slots_ref[0])
    pair_ref[1] = read(slots_ref[1])
    for k in range(half, domains):
        far_refs[k - half][0] = read(slots_ref[2 * k + 2])
    for k in range(1, half):
        near_refs[k - 1][0] = read(slots_ref[2 * k + 1])
        near_refs[k - 1][1] = read(slots_ref[2 * k + 2])


def first_kernel(
    domains, rows, tiles_ref, mig_ref, x_ref, table_ref, slots_ref, which_ref, own_ref, *refs
):
    sends, sem = refs[:-1], refs[-1]
    load = pltpu.make_async_copy(x_ref, own_ref, sem)
    load.start()
    half = domains // 2
    me = lax.axis_index("dom")
    mine0, mine1 = mig_ref[0, me], mig_ref[1, me]
    slots_ref[0] = mine0
    slots_ref[1] = mine1
    opposite = me ^ half
    opposite_last = opposite * rows + mig_ref[1, opposite]

    named = tiles_ref[...]
    user = lax.broadcasted_iota(I32, named.shape, 1) // rows
    slot = named - me * rows
    leaves = (slot == mine0) | (slot == mine1)
    staying = jnp.where((slot >= 0) & (slot < rows) & jnp.logical_not(leaves), slot, 0)
    last = jnp.where(slot == mine1, 1, 0)
    relayed = jnp.where(named == opposite_last, 1, 0)

    def requests(k):
        asks = user == (me ^ k)
        slots_ref[2 * k + 2] = jnp.max(jnp.where(asks, staying, 0))
        slots_ref[2 * k + 1] = jnp.where(jnp.max(jnp.where(asks, last, 0)) == 1, mine1, mine0)
        which_ref[k] = jnp.max(jnp.where(asks, relayed, 0))

    if domains <= 16:
        for k in range(1, domains):
            requests(k)
    else:
        pl.loop(1, domains)(requests)
    load.wait()
    write_sends(domains, slots_ref, lambda s: own_ref[s], sends[0], sends[1:half], sends[half:])

    holder = named // rows
    slot = named - holder * rows
    flip = holder ^ user

    def mark(q, carry):
        first, last = carry
        here = holder == q
        first = first | (here & (slot == mig_ref[0, q])).astype(I32)
        last = last | (here & (slot == mig_ref[1, q])).astype(I32)
        return first, last

    zeros = jnp.zeros_like(named)
    first, last = lax.fori_loop(0, domains, mark, (zeros, zeros))
    leaves = first | last
    place = rows + 2 * flip + 1 - leaves
    place = jnp.where((flip == half) & (leaves == 1), rows + last, place)
    table_ref[...] = jnp.where(flip == 0, slot, place)


def load_kernel(after_ref, *refs):
    del after_ref
    count = len(refs) // 3
    sources, targets, sems = refs[:count], refs[count : 2 * count], refs[2 * count :]
    copies = [pltpu.make_async_copy(*args) for args in zip(sources, targets, sems)]
    for copy in copies:
        copy.start()
    for copy in copies:
        copy.wait()


def relay_kernel(half, which_ref, pair_ref, *outs):
    for k in range(1, half):
        outs[k - 1][0] = pair_ref[which_ref[k]]


def fill_pool(domains, chunks, pair_ref, near_refs, far_refs, relay_refs, pool_ref):
    half = domains // 2
    per = chunks[0].shape[0]
    rows = per * len(chunks)
    if len(chunks) == 1:
        pool_ref[0:rows] = chunks[0][...]
    else:
        feat = lax.axis_index("feat")
        for j, chunk in enumerate(chunks):
            for i in range(per):
                pool_ref[(feat ^ j) * per + i] = chunk[i]
    pool_ref[rows : rows + 2] = pair_ref[...]
    for k in range(1, half):
        pool_ref[rows + 2 * k : rows + 2 * k + 2] = near_refs[k - 1][...]
    for k in range(half, domains):
        pool_ref[rows + 2 * k + 1] = far_refs[k - half][0]
        if k > half:
            pool_ref[rows + 2 * k] = relay_refs[k - half - 1][0]


def sum_row(r, table_ref, adjacency_ref, pool_ref):
    rows, tiles = adjacency_ref.shape[:2]
    g = lax.axis_index("dom") * rows + r
    total = None
    for t in range(0, tiles, 2):
        left = jnp.concatenate([adjacency_ref[r, t], adjacency_ref[r, t + 1]], axis=1)
        right = jnp.concatenate(
            [pool_ref[table_ref[t, g]], pool_ref[table_ref[t + 1, g]]], axis=0
        )
        part = jnp.dot(left, right, preferred_element_type=F32)
        total = part if total is None else total + part
    return total.astype(BF16)


def split_refs(domains, n_chunks, refs):
    half = domains // 2
    chunks, refs = refs[:n_chunks], refs[n_chunks:]
    pair, refs = refs[0], refs[1:]
    near, refs = refs[: half - 1], refs[half - 1 :]
    far, refs = refs[:half], refs[half:]
    relay, rest = refs[: half - 1], refs[half - 1 :]
    return chunks, pair, near, far, relay, rest


def aggregate_first_kernel(domains, feats, table_ref, adjacency_ref, *refs):
    chunks, pair, near, far, relay, rest = split_refs(domains, 1, refs)
    outs, pool_ref = rest[:-1], rest[-1]
    fill_pool(domains, chunks, pair, near, far, relay, pool_ref)
    feat = lax.axis_index("feat")
    per = adjacency_ref.shape[0] // feats
    for j in range(feats):

        @pl.loop(0, per)
        def _(i, j=j):
            outs[j][i] = sum_row((feat ^ j) * per + i, table_ref, adjacency_ref, pool_ref)


def aggregate_leaving_kernel(domains, feats, table_ref, slots_ref, adjacency_ref, *refs):
    chunks, pair, near, far, relay, rest = split_refs(domains, feats, refs)
    out_ref, pool_ref = rest
    fill_pool(domains, chunks, pair, near, far, relay, pool_ref)

    @pl.loop(0, out_ref.shape[0])
    def _(i):
        out_ref[i] = sum_row(slots_ref[i], table_ref, adjacency_ref, pool_ref)


def aggregate_staying_kernel(domains, feats, table_ref, slots_ref, adjacency_ref, *refs):
    chunks, pair, near, far, relay, rest = split_refs(domains, feats, refs)
    out_ref, pool_ref = rest
    fill_pool(domains, chunks, pair, near, far, relay, pool_ref)

    @pl.loop(0, out_ref.shape[0])
    def _(r):
        @pl.when((r != slots_ref[0]) & (r != slots_ref[1]))
        def _():
            out_ref[r] = sum_row(r, table_ref, adjacency_ref, pool_ref)


def dense_kernel(feats, weight_one_ref, weight_two_ref, *refs):
    parts, outs, hidden_ref = refs[:feats], refs[feats : 2 * feats], refs[2 * feats]
    feat = lax.axis_index("feat")
    rows = parts[0].shape[0]
    width = parts[0].shape[1]
    columns = weight_one_ref.shape[1]
    for c in range(0, columns, width):
        total = None
        for j in range(feats):
            start = pl.multiple_of((feat ^ j) * width, width)
            part = jnp.dot(
                parts[j][...],
                weight_one_ref[pl.ds(start, width), c : c + width],
                preferred_element_type=F32,
            )
            total = part if total is None else total + part
        hidden_ref[:, c : c + width] = jnp.maximum(total, 0.0).astype(BF16)
    for j in range(feats):
        start = pl.multiple_of((feat ^ j) * width, width)
        outs[j][...] = jnp.dot(
            hidden_ref[...],
            weight_two_ref[:, pl.ds(start, width)],
            preferred_element_type=F32,
        ).astype(BF16)


def second_kernel(domains, feats, slots_ref, *refs):
    chunks, sends = refs[:feats], refs[feats:]
    half = domains // 2
    own_ref = sends[-1]
    sends = sends[:-1]
    per = chunks[0].shape[0]
    feat = lax.axis_index("feat")
    for j, chunk in enumerate(chunks):
        for i in range(per):
            own_ref[(feat ^ j) * per + i] = chunk[i]
    write_sends(domains, slots_ref, lambda s: own_ref[s], sends[0], sends[1:half], sends[half:])


def place_kernel(slots_ref, moved_ref, out_in_ref, out_ref, sems):
    del out_in_ref
    copies = [
        pltpu.make_async_copy(moved_ref.at[i], out_ref.at[slots_ref[i]], sems.at[i])
        for i in range(moved_ref.shape[0])
    ]
    for copy in copies:
        copy.start()
    for copy in copies:
        copy.wait()


def call(kernel, name, out_shape, in_specs, out_specs, scratch=(), flops=0, moved=0, **kwargs):
    run = pl.pallas_call(
        kernel,
        name=name,
        out_shape=out_shape,
        in_specs=in_specs,
        out_specs=out_specs,
        scratch_shapes=list(scratch),
        cost_estimate=pl.CostEstimate(flops=flops, bytes_accessed=moved, transcendentals=0),
        compiler_params=pltpu.CompilerParams(vmem_limit_bytes=16 << 20),
        **kwargs,
    )

    def apply(*args):
        placed = [
            a
            if spec in (SMEM, ANY)
            else pltpu.with_memory_space_constraint(a, spec.memory_space)
            for a, spec in zip(args, in_specs, strict=True)
        ]
        return run(*placed)

    return apply


def send_shapes(domains, size, width):
    half = domains // 2
    return (
        [block((2, size, width))]
        + [block((2, size, width))] * (half - 1)
        + [block((1, size, width))] * half
    )


def exchange(domains, sends, which, size, width, name):
    half = domains // 2
    pair = swap(sends[0], "dom", half)
    far = [swap(sends[k], "dom", k) for k in range(half, domains)]
    near = [swap(sends[k], "dom", k) for k in range(1, half)]
    relayed = call(
        functools.partial(relay_kernel, half),
        name,
        [block((1, size, width))] * (half - 1),
        [SMEM, VMEM],
        [VMEM] * (half - 1),
        moved=4 * size * width * (half - 1),
    )(which, pair)
    relay = [swap(relayed[k - 1], "dom", k) for k in range(1, half)]
    return [pair, *near, *far, *relay]


def on_device(features, adjacency, tile_src, mig_slot, weight_one, weight_two):
    domains = lax.axis_size("dom")
    feats = lax.axis_size("feat")
    half = domains // 2
    rows, tiles, size, _ = adjacency.shape
    width = features.shape[1]
    per = rows // feats
    blocks = features.reshape(rows, size, width)
    n_sends = domains
    pool = pltpu.VMEM((rows + 2 * domains, size, width), BF16)
    work = 2 * rows * tiles * size * size * width
    read = adjacency.size * 2

    table, slots, which, own, *sends = call(
        functools.partial(first_kernel, domains, rows),
        "first_sends",
        [
            block(tile_src.shape[::-1], I32),
            jax.ShapeDtypeStruct((2 * domains + 1,), I32),
            jax.ShapeDtypeStruct((domains,), I32),
            block((rows, size, width)),
        ]
        + send_shapes(domains, size, width),
        [VMEM, SMEM, HBM],
        [VMEM, SMEM, SMEM] + [VMEM] * (1 + n_sends),
        [pltpu.SemaphoreType.DMA(())],
        moved=4 * size * width * 2 * domains,
    )(tile_src.T, mig_slot.T, blocks)
    adjacency = call(
        load_kernel,
        "load",
        [block(adjacency.shape)],
        [SMEM, HBM],
        [VMEM],
        [pltpu.SemaphoreType.DMA(())],
        moved=read,
    )(which, adjacency)[0]
    arrived = exchange(domains, sends, which, size, width, "first_relay")

    parts = call(
        functools.partial(aggregate_first_kernel, domains, feats),
        "first_sum",
        [block((per, size, width))] * feats,
        [SMEM] + [VMEM] * (2 + len(arrived)),
        [VMEM] * feats,
        [pool],
        flops=work,
        moved=read,
    )(table, adjacency, own, *arrived)
    parts = [p.reshape(per * size, width) for p in parts]
    parts = [parts[0]] + [swap(parts[j], "feat", j) for j in range(1, feats)]

    chunks = call(
        functools.partial(dense_kernel, feats),
        "dense",
        [block((per * size, width))] * feats,
        [VMEM] * (2 + feats),
        [VMEM] * feats,
        [pltpu.VMEM((per * size, weight_one.shape[1]), BF16)],
        flops=4 * per * size * weight_one.size,
        moved=weight_one.size * 4,
    )(weight_one, weight_two, *parts)
    chunks = [chunks[0]] + [swap(chunks[j], "feat", j) for j in range(1, feats)]
    chunks = [c.reshape(per, size, width) for c in chunks]

    sends = call(
        functools.partial(second_kernel, domains, feats),
        "second_sends",
        send_shapes(domains, size, width),
        [SMEM] + [VMEM] * feats,
        [VMEM] * n_sends,
        [pltpu.VMEM((rows, size, width), BF16)],
        moved=4 * size * width * 2 * domains,
    )(slots, *chunks)
    arrived = exchange(domains, sends, which, size, width, "second_relay")

    leaving = call(
        functools.partial(aggregate_leaving_kernel, domains, feats),
        "leaving_sum",
        block((2, size, width)),
        [SMEM, SMEM] + [VMEM] * (1 + feats + len(arrived)),
        VMEM,
        [pool],
        flops=work // 4,
        moved=read // 4,
    )(table, slots, adjacency, *chunks, *arrived)
    moved = lax.ppermute(leaving, "dom", [(i, (i + 1) % domains) for i in range(domains)])
    out = call(
        functools.partial(aggregate_staying_kernel, domains, feats),
        "staying_sum",
        jax.ShapeDtypeStruct((rows, size, width), BF16),
        [SMEM, SMEM] + [VMEM] * (1 + feats + len(arrived)),
        VMEM,
        [pool],
        flops=work * 3 // 4,
        moved=read * 3 // 4,
    )(table, slots, adjacency, *chunks, *arrived)
    out = call(
        place_kernel,
        "place",
        jax.ShapeDtypeStruct((rows, size, width), BF16),
        [SMEM, VMEM, ANY],
        ANY,
        [pltpu.SemaphoreType.DMA((2,))],
        moved=4 * size * width * 2,
        input_output_aliases={2: 0},
    )(slots, moved, out)
    return out.reshape(rows * size, width)


def solution(mesh):
    in_specs = (P("dom", "feat"), P("dom", None, None, None), P(), P(), P(), P())
    return jax.shard_map(
        on_device, mesh=mesh, in_specs=in_specs, out_specs=P("dom", "feat"), check_vma=False
    )
```

```python
import functools

import jax
import jax.numpy as jnp
from jax import lax
from jax.experimental import pallas as pl
from jax.experimental.pallas import tpu as pltpu
from jax.sharding import PartitionSpec as P


BF16 = jnp.bfloat16
F32 = jnp.float32
I32 = jnp.int32
VMEM = pl.BlockSpec(memory_space=pltpu.VMEM)
SMEM = pl.BlockSpec(memory_space=pltpu.SMEM)
ANY = pl.BlockSpec(memory_space=pl.ANY)
HBM = pl.BlockSpec(memory_space=pltpu.HBM)


def swap(value, axis, flip):
    return lax.ppermute(value, axis, [(i, i ^ flip) for i in range(lax.axis_size(axis))])


def block(shape, dtype=BF16):
    return pltpu.VMEM(shape, dtype)


def copy_all(*triples):
    copies = [pltpu.make_async_copy(*triple) for triple in triples]
    for copy in copies:
        copy.start()
    for copy in copies:
        copy.wait()


def pair_kernel(mig_ref, x_ref, pair_ref, mig, sems):
    copy_all((mig_ref, mig, sems.at[0]))
    me = lax.axis_index("dom")
    copy_all(*[(x_ref.at[mig[m, me]], pair_ref.at[m], sems.at[m]) for m in range(2)])


def write_sends(domains, slots_ref, own_ref, near_refs, far_refs):
    half = domains // 2
    for k in range(1, half):
        near_refs[k - 1][0] = own_ref[slots_ref[2 * k]]
        near_refs[k - 1][1] = own_ref[slots_ref[2 * k + 1]]
    for k in range(half, domains):
        far_refs[k - half][0] = own_ref[slots_ref[2 * k + 1]]


def first_kernel(domains, rows, tiles_ref, mig_ref, x_ref, slots_ref, which_ref, own_ref, *refs):
    *sends, tiles, mig, sems = refs
    half = domains // 2
    loads = [
        pltpu.make_async_copy(*triple)
        for triple in (
            (tiles_ref, tiles, sems.at[0]),
            (mig_ref, mig, sems.at[1]),
            (x_ref, own_ref, sems.at[2]),
        )
    ]
    for load in loads:
        load.start()
    for load in loads[:2]:
        load.wait()
    me = lax.axis_index("dom")
    mine0, mine1 = mig[0, me], mig[1, me]
    slots_ref[0] = mine0
    slots_ref[1] = mine1
    opposite = me ^ half
    opposite_last = opposite * rows + mig[1, opposite]

    named = tiles[...]
    user = lax.broadcasted_iota(I32, named.shape, 1) // rows
    slot = named - me * rows
    leaves = (slot == mine0) | (slot == mine1)
    staying = jnp.where((slot >= 0) & (slot < rows) & jnp.logical_not(leaves), slot, 0)
    last = jnp.where(slot == mine1, 1, 0)
    relayed = jnp.where(named == opposite_last, 1, 0)

    def requests(k):
        asks = user == (me ^ k)
        slots_ref[2 * k + 1] = jnp.max(jnp.where(asks, staying, 0))
        slots_ref[2 * k] = jnp.where(jnp.max(jnp.where(asks, last, 0)) == 1, mine1, mine0)
        which_ref[k] = jnp.max(jnp.where(asks, relayed, 0))

    if domains <= 16:
        for k in range(1, domains):
            requests(k)
    else:
        pl.loop(1, domains)(requests)
    loads[2].wait()
    write_sends(domains, slots_ref, own_ref, sends[: half - 1], sends[half - 1 :])


def table_kernel(
    domains, rows, after_ref, tiles_ref, mig_ref, adjacency_ref, table_ref, held_ref, *refs
):
    del after_ref
    tiles, mig, sems = refs
    load = pltpu.make_async_copy(adjacency_ref, held_ref, sems.at[2])
    load.start()
    copy_all((tiles_ref, tiles, sems.at[0]), (mig_ref, mig, sems.at[1]))
    half = domains // 2
    named = tiles[...]
    user = lax.broadcasted_iota(I32, named.shape, 1) // rows
    holder = named // rows
    slot = named - holder * rows
    flip = holder ^ user

    def mark(q, carry):
        first, last = carry
        here = holder == q
        first = first | (here & (slot == mig[0, q])).astype(I32)
        last = last | (here & (slot == mig[1, q])).astype(I32)
        return first, last

    zeros = jnp.zeros_like(named)
    first, last = lax.fori_loop(0, domains, mark, (zeros, zeros))
    leaves = first | last
    place = rows + 2 * flip + 1 - leaves
    place = jnp.where((flip == half) & (leaves == 1), rows + last, place)
    table_ref[...] = jnp.where(flip == 0, slot, place)
    load.wait()


def relay_kernel(half, which_ref, pair_ref, near_ref, first_ref, *outs):
    first_ref[0:2] = near_ref[...]
    first_ref[2] = pair_ref[which_ref[1]]
    for k in range(2, half):
        outs[k - 2][0] = pair_ref[which_ref[k]]


def fill_pool(domains, chunks, arrived, pool_ref):
    half = domains // 2
    per = chunks[0].shape[0]
    rows = per * len(chunks)
    if len(chunks) == 1:
        pool_ref[0:rows] = chunks[0][...]
    else:
        feat = lax.axis_index("feat")
        for j, chunk in enumerate(chunks):
            for i in range(per):
                pool_ref[(feat ^ j) * per + i] = chunk[i]
    pair, near, far, relay = split_arrived(half, arrived)
    pool_ref[rows : rows + 2] = pair[...]
    for k in range(1, half):
        pool_ref[rows + 2 * k : rows + 2 * k + 2] = near[k - 1][0:2]
    pool_ref[rows + 2 * (half + 1)] = near[0][2]
    for k in range(half, domains):
        pool_ref[rows + 2 * k + 1] = far[k - half][0]
    for k in range(2, half):
        pool_ref[rows + 2 * (half + k)] = relay[k - 2][0]


def split_arrived(half, arrived):
    cuts = (1, half, 2 * half)
    pair, near, far, relay = (arrived[i:j] for i, j in zip((0,) + cuts, cuts + (None,)))
    return pair[0], near, far, relay


def sum_row(r, table_ref, adjacency_ref, pool_ref):
    rows, tiles = adjacency_ref.shape[:2]
    g = lax.axis_index("dom") * rows + r
    total = None
    for t in range(0, tiles, 2):
        left = jnp.concatenate([adjacency_ref[r, t], adjacency_ref[r, t + 1]], axis=1)
        right = jnp.concatenate(
            [pool_ref[table_ref[t, g]], pool_ref[table_ref[t + 1, g]]], axis=0
        )
        part = jnp.dot(left, right, preferred_element_type=F32)
        total = part if total is None else total + part
    return total.astype(BF16)


def first_sum_kernel(domains, feats, j, table_ref, adjacency_ref, own_ref, *refs):
    *arrived, pool_ref, out_ref = refs
    fill_pool(domains, [own_ref], arrived, pool_ref)
    sum_part(feats, j, table_ref, adjacency_ref, pool_ref, out_ref)


def part_sum_kernel(feats, js, table_ref, adjacency_ref, pool_ref, *outs):
    for j, out_ref in zip(js, outs, strict=True):
        sum_part(feats, j, table_ref, adjacency_ref, pool_ref, out_ref)


def sum_part(feats, j, table_ref, adjacency_ref, pool_ref, out_ref):
    start = (lax.axis_index("feat") ^ j) * (adjacency_ref.shape[0] // feats)

    @pl.loop(0, out_ref.shape[0])
    def _(i):
        out_ref[i] = sum_row(start + i, table_ref, adjacency_ref, pool_ref)


def leaving_sum_kernel(domains, feats, table_ref, slots_ref, adjacency_ref, *refs):
    *blocks, pool_ref, out_ref = refs
    fill_pool(domains, blocks[:feats], blocks[feats:], pool_ref)

    @pl.loop(0, out_ref.shape[0])
    def _(i):
        out_ref[i] = sum_row(slots_ref[i], table_ref, adjacency_ref, pool_ref)


def staying_sum_kernel(table_ref, slots_ref, adjacency_ref, pool_ref, out_ref):
    @pl.loop(0, out_ref.shape[0])
    def _(r):
        @pl.when((r != slots_ref[0]) & (r != slots_ref[1]))
        def _():
            out_ref[r] = sum_row(r, table_ref, adjacency_ref, pool_ref)


def dense_kernel(feats, weight_one_ref, weight_two_ref, *refs):
    parts, outs, hidden_ref = refs[:feats], refs[feats : 2 * feats], refs[2 * feats]
    feat = lax.axis_index("feat")
    width = parts[0].shape[1]
    columns = weight_one_ref.shape[1]
    for c in range(0, columns, width):
        total = None
        for j in range(feats):
            start = pl.multiple_of((feat ^ j) * width, width)
            part = jnp.dot(
                parts[j][...],
                weight_one_ref[pl.ds(start, width), c : c + width],
                preferred_element_type=F32,
            )
            total = part if total is None else total + part
        hidden_ref[:, c : c + width] = jnp.maximum(total, 0.0).astype(BF16)
    for j in range(feats):
        start = pl.multiple_of((feat ^ j) * width, width)
        outs[j][...] = jnp.dot(
            hidden_ref[...],
            weight_two_ref[:, pl.ds(start, width)],
            preferred_element_type=F32,
        ).astype(BF16)


def second_kernel(domains, feats, slots_ref, *refs):
    chunks, pair_ref, sends, own_ref = refs[:feats], refs[feats], refs[feats + 1 : -1], refs[-1]
    half = domains // 2
    per = chunks[0].shape[0]
    feat = lax.axis_index("feat")
    for j, chunk in enumerate(chunks):
        for i in range(per):
            own_ref[(feat ^ j) * per + i] = chunk[i]
    for m in range(2):
        pair_ref[m] = own_ref[slots_ref[m]]
    write_sends(domains, slots_ref, own_ref, sends[: half - 1], sends[half - 1 :])


def place_kernel(slots_ref, moved_ref, out_in_ref, out_ref, sems):
    del out_in_ref
    copies = [
        pltpu.make_async_copy(moved_ref.at[i], out_ref.at[slots_ref[i]], sems.at[i])
        for i in range(moved_ref.shape[0])
    ]
    for copy in copies:
        copy.start()
    for copy in copies:
        copy.wait()


def call(kernel, out_shape, in_specs, out_specs, scratch=(), flops=0, moved=0, **kwargs):
    run = pl.pallas_call(
        kernel,
        out_shape=out_shape,
        in_specs=in_specs,
        out_specs=out_specs,
        scratch_shapes=list(scratch),
        cost_estimate=pl.CostEstimate(flops=flops, bytes_accessed=moved, transcendentals=0),
        compiler_params=pltpu.CompilerParams(vmem_limit_bytes=16 << 20),
        **kwargs,
    )

    def place_and_run(*args):
        placed = [
            a
            if spec in (SMEM, ANY)
            else pltpu.with_memory_space_constraint(a, spec.memory_space)
            for a, spec in zip(args, in_specs, strict=True)
        ]
        return run(*placed)

    return place_and_run


def exchange(domains, pair, sends, which):
    half = domains // 2
    shape = pair.shape[1:]
    near, far = sends[: half - 1], sends[half - 1 :]
    pair = swap(pair, "dom", half)
    near_z = [swap(near[k - 1], "dom", k) for k in range(2, half)]
    far = [swap(far[k - half], "dom", k) for k in range(half, domains)]
    first, *relay = call(
        functools.partial(relay_kernel, half),
        [block((3, *shape))] + [block((1, *shape))] * (half - 2),
        [SMEM, VMEM, VMEM],
        [VMEM] * (half - 1),
        moved=4 * pair.size * half,
    )(which, pair, near[0])
    relay = [swap(relay[k - 2], "dom", k) for k in range(2, half)]
    return [pair, swap(first, "dom", 1), *near_z, *far, *relay]


def on_device(features, adjacency, tile_src, mig_slot, weight_one, weight_two):
    domains = lax.axis_size("dom")
    feats = lax.axis_size("feat")
    half = domains // 2
    rows, tiles, size, _ = adjacency.shape
    width = features.shape[1]
    per = rows // feats
    blocks = features.reshape(rows, size, width)
    named, leaving_slots = tile_src.T, mig_slot.T
    near_far = [block((2, size, width))] * (half - 1) + [block((1, size, width))] * half
    pool = block((rows + 2 * domains, size, width))
    work = 2 * tiles * size * size * width
    read = adjacency.size * 2 // rows
    tables = [pltpu.VMEM(named.shape, I32), pltpu.SMEM(leaving_slots.shape, I32)]
    sems = pltpu.SemaphoreType.DMA((3,))

    pair = call(
        pair_kernel,
        [block((2, size, width))],
        [HBM, HBM],
        [VMEM],
        [tables[1], sems],
        moved=8 * size * width,
    )(leaving_slots, blocks)[0]
    slots, which, own, *sends = call(
        functools.partial(first_kernel, domains, rows),
        [
            jax.ShapeDtypeStruct((2 * domains,), I32),
            jax.ShapeDtypeStruct((domains,), I32),
            block((rows, size, width)),
            *near_far,
        ],
        [HBM, HBM, HBM],
        [SMEM, SMEM] + [VMEM] * (1 + len(near_far)),
        [*tables, sems],
        moved=8 * size * width * domains,
    )(named, leaving_slots, blocks)
    arrived = exchange(domains, pair, sends, which)
    table, adjacency = call(
        functools.partial(table_kernel, domains, rows),
        [block(named.shape, I32), block(adjacency.shape)],
        [SMEM, HBM, HBM, HBM],
        [VMEM, VMEM],
        [*tables, sems],
        moved=adjacency.size * 2,
    )(which, named, leaving_slots, adjacency)

    early = list(range(2, feats))
    parts = [None] * feats
    pool_one, parts[2] = call(
        functools.partial(first_sum_kernel, domains, feats, 2),
        [pool, block((per, size, width))],
        [SMEM] + [VMEM] * (2 + len(arrived)),
        [VMEM] * 2,
        flops=work * per,
        moved=read * per,
    )(table, adjacency, own, *arrived)
    for js in [[j] for j in early[1:]] + [[1, 0]]:
        outs = call(
            functools.partial(part_sum_kernel, feats, js),
            [block((per, size, width))] * len(js),
            [SMEM, VMEM, VMEM],
            [VMEM] * len(js),
            flops=work * per * len(js),
            moved=read * per * len(js),
        )(table, adjacency, pool_one)
        for j, out in zip(js, outs):
            parts[j] = out
    parts = [p.reshape(per * size, width) for p in parts]
    parts = [p if j == 0 else swap(p, "feat", j) for j, p in enumerate(parts)]

    chunks = call(
        functools.partial(dense_kernel, feats),
        [block((per * size, width))] * feats,
        [VMEM] * (2 + feats),
        [VMEM] * feats,
        [pltpu.VMEM((per * size, weight_one.shape[1]), BF16)],
        flops=4 * per * size * weight_one.size,
        moved=weight_one.size * 4,
    )(weight_one, weight_two, *parts)
    chunks = [c if j == 0 else swap(c, "feat", j) for j, c in enumerate(chunks)]
    chunks = [c.reshape(per, size, width) for c in chunks]

    pair, *sends = call(
        functools.partial(second_kernel, domains, feats),
        [block((2, size, width)), *near_far],
        [SMEM] + [VMEM] * feats,
        [VMEM] * (1 + len(near_far)),
        [pltpu.VMEM((rows, size, width), BF16)],
        moved=8 * size * width * domains,
    )(slots, *chunks)
    arrived = exchange(domains, pair, sends, which)

    pool_two, leaving = call(
        functools.partial(leaving_sum_kernel, domains, feats),
        [pool, block((2, size, width))],
        [SMEM, SMEM] + [VMEM] * (1 + feats + len(arrived)),
        [VMEM] * 2,
        flops=work * 2,
        moved=read * 2,
    )(table, slots, adjacency, *chunks, *arrived)
    moved = lax.ppermute(leaving, "dom", [(i, (i + 1) % domains) for i in range(domains)])
    out = call(
        staying_sum_kernel,
        jax.ShapeDtypeStruct((rows, size, width), BF16),
        [SMEM, SMEM, VMEM, VMEM],
        VMEM,
        flops=work * (rows - 2),
        moved=read * (rows - 2),
    )(table, slots, adjacency, pool_two)
    out = call(
        place_kernel,
        jax.ShapeDtypeStruct((rows, size, width), BF16),
        [SMEM, VMEM, ANY],
        ANY,
        [pltpu.SemaphoreType.DMA((2,))],
        moved=4 * size * width * 2,
        input_output_aliases={2: 0},
    )(slots, moved, out)
    return out.reshape(rows * size, width)


def solution(mesh):
    in_specs = (P("dom", "feat"), P("dom", None, None, None), P(), P(), P(), P())
    return jax.shard_map(
        on_device, mesh=mesh, in_specs=in_specs, out_specs=P("dom", "feat"), check_vma=False
    )
```

```python
import functools

import jax
import jax.numpy as jnp
from jax import lax
from jax.experimental import pallas as pl
from jax.experimental.pallas import tpu as pltpu
from jax.sharding import PartitionSpec as P


BF16 = jnp.bfloat16
F32 = jnp.float32
I32 = jnp.int32
VMEM = pl.BlockSpec(memory_space=pltpu.VMEM)
SMEM = pl.BlockSpec(memory_space=pltpu.SMEM)
ANY = pl.BlockSpec(memory_space=pl.ANY)
HBM = pl.BlockSpec(memory_space=pltpu.HBM)


def swap(value, axis, flip):
    return lax.ppermute(value, axis, [(i, i ^ flip) for i in range(lax.axis_size(axis))])


def block(shape, dtype=BF16):
    return pltpu.VMEM(shape, dtype)


def scalars(shape):
    return pltpu.SMEM(shape, I32)


def copy_all(*triples):
    copies = [pltpu.make_async_copy(*triple) for triple in triples]
    for copy in copies:
        copy.start()
    for copy in copies:
        copy.wait()


def load_kernel(tiles_ref, mig_ref, x_ref, named_ref, slots_ref, own_ref, pair_ref, sems):
    copy_all(
        (tiles_ref, named_ref, sems.at[0]),
        (mig_ref, slots_ref, sems.at[1]),
        (x_ref, own_ref, sems.at[2]),
    )
    me = lax.axis_index("dom")
    for m in range(2):
        pair_ref[m] = own_ref[slots_ref[m, me]]


def write_sends(domains, slots_ref, own_ref, near_refs, far_refs):
    half = domains // 2
    for k in range(1, half):
        near_refs[k - 1][0] = own_ref[slots_ref[2 * k]]
        near_refs[k - 1][1] = own_ref[slots_ref[2 * k + 1]]
    for k in range(half, domains):
        far_refs[k - half][0] = own_ref[slots_ref[2 * k + 1]]


def first_kernel(domains, rows, mig, tiles_ref, own_ref, slots_ref, which_ref, *sends):
    half = domains // 2
    me = lax.axis_index("dom")
    mine0, mine1 = mig[0, me], mig[1, me]
    slots_ref[0] = mine0
    slots_ref[1] = mine1
    opposite = me ^ half
    opposite_last = opposite * rows + mig[1, opposite]

    named = tiles_ref[...]
    user = lax.broadcasted_iota(I32, named.shape, 1) // rows
    slot = named - me * rows
    leaves = (slot == mine0) | (slot == mine1)
    staying = jnp.where((slot >= 0) & (slot < rows) & jnp.logical_not(leaves), slot, 0)
    last = jnp.where(slot == mine1, 1, 0)
    relayed = jnp.where(named == opposite_last, 1, 0)

    def requests(k):
        asks = user == (me ^ k)
        slots_ref[2 * k + 1] = jnp.max(jnp.where(asks, staying, 0))
        slots_ref[2 * k] = jnp.where(jnp.max(jnp.where(asks, last, 0)) == 1, mine1, mine0)
        which_ref[k] = jnp.max(jnp.where(asks, relayed, 0))

    if domains <= 16:
        for k in range(1, domains):
            requests(k)
    else:
        pl.loop(1, domains)(requests)
    write_sends(domains, slots_ref, own_ref, sends[: half - 1], sends[half - 1 :])


def table_kernel(
    domains, rows, mig, tiles_ref, adjacency_ref, table_ref, held_ref, found_ref, sems
):
    load = pltpu.make_async_copy(adjacency_ref, held_ref, sems.at[0])
    load.start()
    half = domains // 2
    named = tiles_ref[...]
    user = lax.broadcasted_iota(I32, named.shape, 1) // rows
    holder = named // rows
    slot = named - holder * rows
    flip = holder ^ user

    def mark(q, carry):
        first, last = carry
        here = holder == q
        first = first | (here & (slot == mig[0, q])).astype(I32)
        last = last | (here & (slot == mig[1, q])).astype(I32)
        return first, last

    zeros = jnp.zeros_like(named)
    first, last = lax.fori_loop(0, domains, mark, (zeros, zeros))
    leaves = first | last
    place = rows + 2 * flip + 1 - leaves
    place = jnp.where((flip == half) & (leaves == 1), rows + last, place)
    found_ref[...] = jnp.where(flip == 0, slot, place)
    copy_all((found_ref, table_ref, sems.at[1]))
    load.wait()


def relay_kernel(half, which_ref, pair_ref, near_ref, first_ref, *outs):
    first_ref[0:2] = near_ref[...]
    first_ref[2] = pair_ref[which_ref[1]]
    for k in range(2, half):
        outs[k - 2][0] = pair_ref[which_ref[k]]


def fill_pool(domains, chunks, arrived, pool_ref):
    half = domains // 2
    per = chunks[0].shape[0]
    rows = per * len(chunks)
    if len(chunks) == 1:
        pool_ref[0:rows] = chunks[0][...]
    else:
        feat = lax.axis_index("feat")
        for j, chunk in enumerate(chunks):
            for i in range(per):
                pool_ref[(feat ^ j) * per + i] = chunk[i]
    pair, near, far, relay = split_arrived(half, arrived)
    pool_ref[rows : rows + 2] = pair[...]
    for k in range(1, half):
        pool_ref[rows + 2 * k : rows + 2 * k + 2] = near[k - 1][0:2]
    pool_ref[rows + 2 * (half + 1)] = near[0][2]
    for k in range(half, domains):
        pool_ref[rows + 2 * k + 1] = far[k - half][0]
    for k in range(2, half):
        pool_ref[rows + 2 * (half + k)] = relay[k - 2][0]


def split_arrived(half, arrived):
    cuts = (1, half, 2 * half)
    pair, near, far, relay = (arrived[i:j] for i, j in zip((0,) + cuts, cuts + (None,)))
    return pair[0], near, far, relay


def sum_row(r, table_ref, adjacency_ref, pool_ref):
    rows, tiles = adjacency_ref.shape[:2]
    g = lax.axis_index("dom") * rows + r
    total = None
    for t in range(0, tiles, 2):
        left = jnp.concatenate([adjacency_ref[r, t], adjacency_ref[r, t + 1]], axis=1)
        right = jnp.concatenate(
            [pool_ref[table_ref[t, g]], pool_ref[table_ref[t + 1, g]]], axis=0
        )
        part = jnp.dot(left, right, preferred_element_type=F32)
        total = part if total is None else total + part
    return total.astype(BF16)


def first_sum_kernel(domains, feats, j, table_ref, adjacency_ref, own_ref, *refs):
    *arrived, pool_ref, out_ref = refs
    fill_pool(domains, [own_ref], arrived, pool_ref)
    sum_part(feats, j, table_ref, adjacency_ref, pool_ref, out_ref)


def part_sum_kernel(feats, js, table_ref, adjacency_ref, pool_ref, *outs):
    for j, out_ref in zip(js, outs, strict=True):
        sum_part(feats, j, table_ref, adjacency_ref, pool_ref, out_ref)


def sum_part(feats, j, table_ref, adjacency_ref, pool_ref, out_ref):
    start = (lax.axis_index("feat") ^ j) * (adjacency_ref.shape[0] // feats)

    @pl.loop(0, out_ref.shape[0])
    def _(i):
        out_ref[i] = sum_row(start + i, table_ref, adjacency_ref, pool_ref)


def leaving_sum_kernel(domains, feats, table_ref, slots_ref, adjacency_ref, *refs):
    *blocks, pool_ref, out_ref = refs
    fill_pool(domains, blocks[:feats], blocks[feats:], pool_ref)

    @pl.loop(0, out_ref.shape[0])
    def _(i):
        out_ref[i] = sum_row(slots_ref[i], table_ref, adjacency_ref, pool_ref)


def staying_sum_kernel(table_ref, slots_ref, adjacency_ref, pool_ref, out_ref):
    @pl.loop(0, out_ref.shape[0])
    def _(r):
        @pl.when((r != slots_ref[0]) & (r != slots_ref[1]))
        def _():
            out_ref[r] = sum_row(r, table_ref, adjacency_ref, pool_ref)


def dense_kernel(feats, weight_one_ref, weight_two_ref, *refs):
    parts, outs, hidden_ref = refs[:feats], refs[feats : 2 * feats], refs[2 * feats]
    feat = lax.axis_index("feat")
    width = parts[0].shape[1]
    columns = weight_one_ref.shape[1]
    for c in range(0, columns, width):
        total = None
        for j in range(feats):
            start = pl.multiple_of((feat ^ j) * width, width)
            part = jnp.dot(
                parts[j][...],
                weight_one_ref[pl.ds(start, width), c : c + width],
                preferred_element_type=F32,
            )
            total = part if total is None else total + part
        hidden_ref[:, c : c + width] = jnp.maximum(total, 0.0).astype(BF16)
    for j in range(feats):
        start = pl.multiple_of((feat ^ j) * width, width)
        outs[j][...] = jnp.dot(
            hidden_ref[...],
            weight_two_ref[:, pl.ds(start, width)],
            preferred_element_type=F32,
        ).astype(BF16)


def second_kernel(domains, feats, slots_ref, *refs):
    chunks, pair_ref, sends, own_ref = refs[:feats], refs[feats], refs[feats + 1 : -1], refs[-1]
    half = domains // 2
    per = chunks[0].shape[0]
    feat = lax.axis_index("feat")
    for j, chunk in enumerate(chunks):
        for i in range(per):
            own_ref[(feat ^ j) * per + i] = chunk[i]
    for m in range(2):
        pair_ref[m] = own_ref[slots_ref[m]]
    write_sends(domains, slots_ref, own_ref, sends[: half - 1], sends[half - 1 :])


def place_kernel(slots_ref, moved_ref, out_in_ref, out_ref, sems):
    del out_in_ref
    copies = [
        pltpu.make_async_copy(moved_ref.at[i], out_ref.at[slots_ref[i]], sems.at[i])
        for i in range(moved_ref.shape[0])
    ]
    for copy in copies:
        copy.start()
    for copy in copies:
        copy.wait()


def call(kernel, out_shape, in_specs, out_specs, scratch=(), flops=0, moved=0, **kwargs):
    run = pl.pallas_call(
        kernel,
        out_shape=out_shape,
        in_specs=in_specs,
        out_specs=out_specs,
        scratch_shapes=list(scratch),
        cost_estimate=pl.CostEstimate(flops=flops, bytes_accessed=moved, transcendentals=0),
        compiler_params=pltpu.CompilerParams(vmem_limit_bytes=16 << 20),
        **kwargs,
    )

    def place_and_run(*args):
        placed = [
            a if spec is ANY else pltpu.with_memory_space_constraint(a, spec.memory_space)
            for a, spec in zip(args, in_specs, strict=True)
        ]
        return run(*placed)

    return place_and_run


def exchange(domains, pair, sends, which):
    half = domains // 2
    shape = pair.shape[1:]
    near, far = sends[: half - 1], sends[half - 1 :]
    pair = swap(pair, "dom", half)
    near_z = [swap(near[k - 1], "dom", k) for k in range(2, half)]
    far = [swap(far[k - half], "dom", k) for k in range(half, domains)]
    first, *relay = call(
        functools.partial(relay_kernel, half),
        [block((3, *shape))] + [block((1, *shape))] * (half - 2),
        [SMEM, VMEM, VMEM],
        [VMEM] * (half - 1),
        moved=4 * pair.size * half,
    )(which, pair, near[0])
    relay = [swap(relay[k - 2], "dom", k) for k in range(2, half)]
    return [pair, swap(first, "dom", 1), *near_z, *far, *relay]


def on_device(features, adjacency, tile_src, mig_slot, weight_one, weight_two):
    domains = lax.axis_size("dom")
    feats = lax.axis_size("feat")
    half = domains // 2
    rows, tiles, size, _ = adjacency.shape
    width = features.shape[1]
    per = rows // feats
    blocks = features.reshape(rows, size, width)
    named, leaving_slots = tile_src.T, mig_slot.T
    near_far = [block((2, size, width))] * (half - 1) + [block((1, size, width))] * half
    pool = block((rows + 2 * domains, size, width))
    work = 2 * tiles * size * size * width
    read = adjacency.size * 2 // rows
    named, mig, own, pair = call(
        load_kernel,
        [
            block(named.shape, I32),
            scalars(leaving_slots.shape),
            block((rows, size, width)),
            block((2, size, width)),
        ],
        [HBM, HBM, HBM],
        [VMEM, SMEM, VMEM, VMEM],
        [pltpu.SemaphoreType.DMA((3,))],
        moved=features.size * 2,
    )(named, leaving_slots, blocks)
    slots, which, *sends = call(
        functools.partial(first_kernel, domains, rows),
        [scalars((2 * domains,)), scalars((domains,)), *near_far],
        [SMEM, VMEM, VMEM],
        [SMEM, SMEM] + [VMEM] * len(near_far),
        moved=8 * size * width * domains,
    )(mig, named, own)
    arrived = exchange(domains, pair, sends, which)
    table, adjacency = call(
        functools.partial(table_kernel, domains, rows),
        [scalars(named.shape), block(adjacency.shape)],
        [SMEM, VMEM, HBM],
        [SMEM, VMEM],
        [pltpu.VMEM(named.shape, I32), pltpu.SemaphoreType.DMA((2,))],
        moved=adjacency.size * 2,
    )(mig, named, adjacency)

    early = list(range(2, feats))
    parts = [None] * feats
    pool_one, parts[2] = call(
        functools.partial(first_sum_kernel, domains, feats, 2),
        [pool, block((per, size, width))],
        [SMEM] + [VMEM] * (2 + len(arrived)),
        [VMEM] * 2,
        flops=work * per,
        moved=read * per,
    )(table, adjacency, own, *arrived)
    for js in [[j] for j in early[1:]] + [[1, 0]]:
        outs = call(
            functools.partial(part_sum_kernel, feats, js),
            [block((per, size, width))] * len(js),
            [SMEM, VMEM, VMEM],
            [VMEM] * len(js),
            flops=work * per * len(js),
            moved=read * per * len(js),
        )(table, adjacency, pool_one)
        for j, out in zip(js, outs):
            parts[j] = out
    parts = [p.reshape(per * size, width) for p in parts]
    parts = [p if j == 0 else swap(p, "feat", j) for j, p in enumerate(parts)]

    chunks = call(
        functools.partial(dense_kernel, feats),
        [block((per * size, width))] * feats,
        [VMEM] * (2 + feats),
        [VMEM] * feats,
        [pltpu.VMEM((per * size, weight_one.shape[1]), BF16)],
        flops=4 * per * size * weight_one.size,
        moved=weight_one.size * 4,
    )(weight_one, weight_two, *parts)
    chunks = [c if j == 0 else swap(c, "feat", j) for j, c in enumerate(chunks)]
    chunks = [c.reshape(per, size, width) for c in chunks]

    pair, *sends = call(
        functools.partial(second_kernel, domains, feats),
        [block((2, size, width)), *near_far],
        [SMEM] + [VMEM] * feats,
        [VMEM] * (1 + len(near_far)),
        [pltpu.VMEM((rows, size, width), BF16)],
        moved=8 * size * width * domains,
    )(slots, *chunks)
    arrived = exchange(domains, pair, sends, which)

    pool_two, leaving = call(
        functools.partial(leaving_sum_kernel, domains, feats),
        [pool, block((2, size, width))],
        [SMEM, SMEM] + [VMEM] * (1 + feats + len(arrived)),
        [VMEM] * 2,
        flops=work * 2,
        moved=read * 2,
    )(table, slots, adjacency, *chunks, *arrived)
    moved = lax.ppermute(leaving, "dom", [(i, (i + 1) % domains) for i in range(domains)])
    out = call(
        staying_sum_kernel,
        jax.ShapeDtypeStruct((rows, size, width), BF16),
        [SMEM, SMEM, VMEM, VMEM],
        VMEM,
        flops=work * (rows - 2),
        moved=read * (rows - 2),
    )(table, slots, adjacency, pool_two)
    out = call(
        place_kernel,
        jax.ShapeDtypeStruct((rows, size, width), BF16),
        [SMEM, VMEM, ANY],
        ANY,
        [pltpu.SemaphoreType.DMA((2,))],
        moved=4 * size * width * 2,
        input_output_aliases={2: 0},
    )(slots, moved, out)
    return out.reshape(rows * size, width)


def solution(mesh):
    in_specs = (P("dom", "feat"), P("dom", None, None, None), P(), P(), P(), P())
    return jax.shard_map(
        on_device, mesh=mesh, in_specs=in_specs, out_specs=P("dom", "feat"), check_vma=False
    )
```

```python
import functools

import jax
import jax.numpy as jnp
from jax import lax
from jax.experimental import pallas as pl
from jax.experimental.pallas import tpu as pltpu
from jax.sharding import PartitionSpec as P


BF16 = jnp.bfloat16
F32 = jnp.float32
I32 = jnp.int32
VMEM = pl.BlockSpec(memory_space=pltpu.VMEM)
SMEM = pl.BlockSpec(memory_space=pltpu.SMEM)
ANY = pl.BlockSpec(memory_space=pl.ANY)
HBM = pl.BlockSpec(memory_space=pltpu.HBM)


def swap(value, axis, flip):
    return lax.ppermute(value, axis, [(i, i ^ flip) for i in range(lax.axis_size(axis))])


def block(shape, dtype=BF16):
    return pltpu.VMEM(shape, dtype)


def scalars(shape):
    return pltpu.SMEM(shape, I32)


def copy_all(*triples):
    copies = [pltpu.make_async_copy(*triple) for triple in triples]
    for copy in copies:
        copy.start()
    for copy in copies:
        copy.wait()


def load_kernel(tiles_ref, mig_ref, x_ref, named_ref, slots_ref, own_ref, pair_ref, sems):
    copy_all(
        (tiles_ref, named_ref, sems.at[0]),
        (mig_ref, slots_ref, sems.at[1]),
        (x_ref, own_ref, sems.at[2]),
    )
    me = lax.axis_index("dom")
    for m in range(2):
        pair_ref[m] = own_ref[slots_ref[m, me]]


def write_sends(domains, slots_ref, own_ref, near_refs, far_refs):
    half = domains // 2
    for k in range(1, half):
        near_refs[k - 1][0] = own_ref[slots_ref[2 * k]]
        near_refs[k - 1][1] = own_ref[slots_ref[2 * k + 1]]
    for k in range(half, domains):
        far_refs[k - half][0] = own_ref[slots_ref[2 * k + 1]]


def first_kernel(domains, rows, mig, tiles_ref, own_ref, slots_ref, which_ref, deal_ref, *sends):
    half = domains // 2
    me = lax.axis_index("dom")
    mine0, mine1 = mig[0, me], mig[1, me]
    slots_ref[0] = mine0
    slots_ref[1] = mine1
    deal_ref[0] = mine0
    deal_ref[1] = mine1
    place = jnp.int32(2)
    for s in range(rows):
        deal_ref[place] = s
        place = place + jnp.where((mine0 == s) | (mine1 == s), 0, 1)
    opposite = me ^ half
    opposite_last = opposite * rows + mig[1, opposite]

    named = tiles_ref[...]
    user = lax.broadcasted_iota(I32, named.shape, 1) // rows
    slot = named - me * rows
    leaves = (slot == mine0) | (slot == mine1)
    staying = jnp.where((slot >= 0) & (slot < rows) & jnp.logical_not(leaves), slot, 0)
    last = jnp.where(slot == mine1, 1, 0)
    relayed = jnp.where(named == opposite_last, 1, 0)

    def requests(k):
        asks = user == (me ^ k)
        slots_ref[2 * k + 1] = jnp.max(jnp.where(asks, staying, 0))
        slots_ref[2 * k] = jnp.where(jnp.max(jnp.where(asks, last, 0)) == 1, mine1, mine0)
        which_ref[k] = jnp.max(jnp.where(asks, relayed, 0))

    if domains <= 16:
        for k in range(1, domains):
            requests(k)
    else:
        pl.loop(1, domains)(requests)
    write_sends(domains, slots_ref, own_ref, sends[: half - 1], sends[half - 1 :])


def table_kernel(
    domains, rows, mig, tiles_ref, adjacency_ref, table_ref, held_ref, found_ref, sems
):
    load = pltpu.make_async_copy(adjacency_ref, held_ref, sems.at[0])
    load.start()
    half = domains // 2
    named = tiles_ref[...]
    user = lax.broadcasted_iota(I32, named.shape, 1) // rows
    holder = named // rows
    slot = named - holder * rows
    flip = holder ^ user

    def mark(q, carry):
        first, last = carry
        here = holder == q
        first = first | (here & (slot == mig[0, q])).astype(I32)
        last = last | (here & (slot == mig[1, q])).astype(I32)
        return first, last

    zeros = jnp.zeros_like(named)
    first, last = lax.fori_loop(0, domains, mark, (zeros, zeros))
    leaves = first | last
    place = rows + 2 * flip + 1 - leaves
    place = jnp.where((flip == half) & (leaves == 1), rows + last, place)
    found_ref[...] = jnp.where(flip == 0, slot, place)
    copy_all((found_ref, table_ref, sems.at[1]))
    load.wait()


def relay_kernel(half, which_ref, pair_ref, *outs):
    for k in range(1, half):
        outs[k - 1][0] = pair_ref[which_ref[k]]


def fill_pool(domains, own_ref, arrived, pool_ref):
    half = domains // 2
    rows = own_ref.shape[0]
    pool_ref[0:rows] = own_ref[...]
    pair, near, far, relay = split_arrived(half, arrived)
    pool_ref[rows : rows + 2] = pair[...]
    for k in range(1, half):
        pool_ref[rows + 2 * k : rows + 2 * k + 2] = near[k - 1][...]
        pool_ref[rows + 2 * (half + k)] = relay[k - 1][0]
    for k in range(half, domains):
        pool_ref[rows + 2 * k + 1] = far[k - half][0]


def split_arrived(half, arrived):
    cuts = (1, half, 2 * half)
    pair, near, far, relay = (arrived[i:j] for i, j in zip((0,) + cuts, cuts + (None,)))
    return pair[0], near, far, relay


def sum_row(r, table_ref, adjacency_ref, pool_ref):
    rows, tiles = adjacency_ref.shape[:2]
    g = lax.axis_index("dom") * rows + r
    total = None
    for t in range(0, tiles, 2):
        left = jnp.concatenate([adjacency_ref[r, t], adjacency_ref[r, t + 1]], axis=1)
        right = jnp.concatenate(
            [pool_ref[table_ref[t, g]], pool_ref[table_ref[t + 1, g]]], axis=0
        )
        part = jnp.dot(left, right, preferred_element_type=F32)
        total = part if total is None else total + part
    return total.astype(BF16)


def first_sum_kernel(domains, feats, j, table_ref, deal_ref, adjacency_ref, own_ref, *refs):
    *arrived, pool_ref, out_ref = refs
    fill_pool(domains, own_ref, arrived, pool_ref)
    part_sum_kernel(feats, [j], table_ref, deal_ref, adjacency_ref, pool_ref, out_ref)


def part_sum_kernel(feats, js, table_ref, deal_ref, adjacency_ref, pool_ref, *outs):
    for j, out_ref in zip(js, outs, strict=True):
        rank = lax.axis_index("feat") ^ j

        @pl.loop(0, out_ref.shape[0])
        def _(i, rank=rank, out_ref=out_ref):
            out_ref[i] = sum_row(deal_ref[i * feats + rank], table_ref, adjacency_ref, pool_ref)


def leaving_sum_kernel(domains, table_ref, slots_ref, adjacency_ref, own_ref, *refs):
    *arrived, pool_ref, out_ref = refs
    fill_pool(domains, own_ref, arrived, pool_ref)

    @pl.loop(0, out_ref.shape[0])
    def _(i):
        out_ref[i] = sum_row(slots_ref[i], table_ref, adjacency_ref, pool_ref)


def staying_sum_kernel(table_ref, slots_ref, adjacency_ref, pool_ref, out_ref):
    @pl.loop(0, out_ref.shape[0])
    def _(r):
        @pl.when((r != slots_ref[0]) & (r != slots_ref[1]))
        def _():
            out_ref[r] = sum_row(r, table_ref, adjacency_ref, pool_ref)


def dense_kernel(feats, chunk, weight_one_ref, weight_two_ref, *refs):
    parts, outs, hidden_ref = refs[:feats], refs[feats : 2 * feats], refs[2 * feats]
    feat = lax.axis_index("feat")
    width = parts[0].shape[2]
    columns = weight_one_ref.shape[1]
    rows = [part[chunk] for part in parts]
    for c in range(0, columns, width):
        total = None
        for j in range(feats):
            start = pl.multiple_of((feat ^ j) * width, width)
            part = jnp.dot(
                rows[j],
                weight_one_ref[pl.ds(start, width), c : c + width],
                preferred_element_type=F32,
            )
            total = part if total is None else total + part
        hidden_ref[:, c : c + width] = jnp.maximum(total, 0.0).astype(BF16)
    for j in range(feats):
        start = pl.multiple_of((feat ^ j) * width, width)
        outs[j][0] = jnp.dot(
            hidden_ref[...],
            weight_two_ref[:, pl.ds(start, width)],
            preferred_element_type=F32,
        ).astype(BF16)


def second_pair_kernel(*refs):
    *blocks, pair_ref = refs
    feat = lax.axis_index("feat")
    for j, ref in enumerate(blocks):

        @pl.when((feat ^ j) < 2)
        def _(j=j, ref=ref):
            pair_ref[feat ^ j] = ref[0]


def second_kernel(domains, feats, slots_ref, deal_ref, *refs):
    half = domains // 2
    n_blocks = len(refs) - 1 - (domains - 1)
    blocks, own_ref, sends = refs[:n_blocks], refs[n_blocks], refs[n_blocks + 1 :]
    feat = lax.axis_index("feat")
    for n, ref in enumerate(blocks):
        i, j = divmod(n, feats)
        own_ref[deal_ref[i * feats + (feat ^ j)]] = ref[0]
    write_sends(domains, slots_ref, own_ref, sends[: half - 1], sends[half - 1 :])


def place_kernel(slots_ref, moved_ref, out_in_ref, out_ref, sems):
    del out_in_ref
    copies = [
        pltpu.make_async_copy(moved_ref.at[i], out_ref.at[slots_ref[i]], sems.at[i])
        for i in range(moved_ref.shape[0])
    ]
    for copy in copies:
        copy.start()
    for copy in copies:
        copy.wait()


def call(body, out_shape, in_specs, out_specs, scratch=(), flops=0, moved=0, **kwargs):
    run = pl.pallas_call(
        body,
        out_shape=out_shape,
        in_specs=in_specs,
        out_specs=out_specs,
        scratch_shapes=list(scratch),
        cost_estimate=pl.CostEstimate(flops=flops, bytes_accessed=moved, transcendentals=0),
        compiler_params=pltpu.CompilerParams(vmem_limit_bytes=16 << 20),
        **kwargs,
    )

    def place_and_run(*args):
        placed = [
            a if spec is ANY else pltpu.with_memory_space_constraint(a, spec.memory_space)
            for a, spec in zip(args, in_specs, strict=True)
        ]
        return run(*placed)

    return place_and_run


def exchange(domains, pair, sends, which):
    half = domains // 2
    shape = pair.shape[1:]
    near, far = sends[: half - 1], sends[half - 1 :]
    pair = swap(pair, "dom", half)
    near = [swap(near[k - 1], "dom", k) for k in range(1, half)]
    far = [swap(far[k - half], "dom", k) for k in range(half, domains)]
    relay = call(
        functools.partial(relay_kernel, half),
        [block((1, *shape))] * (half - 1),
        [SMEM, VMEM],
        [VMEM] * (half - 1),
        moved=4 * pair.size * half,
    )(which, pair)
    relay = [swap(relay[k - 1], "dom", k) for k in range(1, half)]
    return [pair, *near, *far, *relay]


def on_device(features, adjacency, tile_src, mig_slot, weight_one, weight_two):
    domains = lax.axis_size("dom")
    feats = lax.axis_size("feat")
    half = domains // 2
    rows, tiles, size, _ = adjacency.shape
    width = features.shape[1]
    per = rows // feats
    blocks = features.reshape(rows, size, width)
    named, leaving_slots = tile_src.T, mig_slot.T
    near_far = [block((2, size, width))] * (half - 1) + [block((1, size, width))] * half
    pool = block((rows + 2 * domains, size, width))
    work = 2 * tiles * size * size * width
    read = adjacency.size * 2 // rows
    named, mig, own, pair = call(
        load_kernel,
        [
            block(named.shape, I32),
            scalars(leaving_slots.shape),
            block((rows, size, width)),
            block((2, size, width)),
        ],
        [HBM, HBM, HBM],
        [VMEM, SMEM, VMEM, VMEM],
        [pltpu.SemaphoreType.DMA((3,))],
        moved=features.size * 2,
    )(named, leaving_slots, blocks)
    slots, which, deal, *sends = call(
        functools.partial(first_kernel, domains, rows),
        [scalars((2 * domains,)), scalars((domains,)), scalars((rows + 1,)), *near_far],
        [SMEM, VMEM, VMEM],
        [SMEM] * 3 + [VMEM] * len(near_far),
        moved=8 * size * width * domains,
    )(mig, named, own)
    arrived = exchange(domains, pair, sends, which)
    table, adjacency = call(
        functools.partial(table_kernel, domains, rows),
        [scalars(named.shape), block(adjacency.shape)],
        [SMEM, VMEM, HBM],
        [SMEM, VMEM],
        [pltpu.VMEM(named.shape, I32), pltpu.SemaphoreType.DMA((2,))],
        moved=adjacency.size * 2,
    )(mig, named, adjacency)

    one = block((1, size, width))
    whole = block((per, size, width))
    parts = [None] * feats
    pool_one, parts[2] = call(
        functools.partial(first_sum_kernel, domains, feats, 2),
        [pool, whole],
        [SMEM, SMEM] + [VMEM] * (2 + len(arrived)),
        [VMEM] * 2,
        flops=work * per,
        moved=read * per,
    )(table, deal, adjacency, own, *arrived)
    for js in [[j] for j in range(3, feats)] + [[1, 0]]:
        outs = call(
            functools.partial(part_sum_kernel, feats, js),
            [whole] * len(js),
            [SMEM, SMEM, VMEM, VMEM],
            [VMEM] * len(js),
            flops=work * per * len(js),
            moved=read * per * len(js),
        )(table, deal, adjacency, pool_one)
        for j, out in zip(js, outs):
            parts[j] = out
    parts = [p if j == 0 else swap(p, "feat", j) for j, p in enumerate(parts)]

    columns = []
    for i in range(per):
        outs = call(
            functools.partial(dense_kernel, feats, i),
            [one] * feats,
            [VMEM] * (2 + feats),
            [VMEM] * feats,
            [pltpu.VMEM((size, weight_one.shape[1]), BF16)],
            flops=4 * size * weight_one.size,
            moved=weight_one.size * 4,
        )(weight_one, weight_two, *parts)
        columns += [c if j == 0 else swap(c, "feat", j) for j, c in enumerate(outs)]

    pair = call(
        second_pair_kernel,
        [block((2, size, width))],
        [VMEM] * feats,
        [VMEM],
        moved=8 * size * width,
    )(*columns[:feats])[0]
    own, *sends = call(
        functools.partial(second_kernel, domains, feats),
        [block((rows, size, width)), *near_far],
        [SMEM, SMEM] + [VMEM] * len(columns),
        [VMEM] * (1 + len(near_far)),
        moved=8 * size * width * domains,
    )(slots, deal, *columns)
    arrived = exchange(domains, pair, sends, which)

    pool_two, leaving = call(
        functools.partial(leaving_sum_kernel, domains),
        [pool, block((2, size, width))],
        [SMEM, SMEM] + [VMEM] * (2 + len(arrived)),
        [VMEM] * 2,
        flops=work * 2,
        moved=read * 2,
    )(table, slots, adjacency, own, *arrived)
    moved = lax.ppermute(leaving, "dom", [(i, (i + 1) % domains) for i in range(domains)])
    out = call(
        staying_sum_kernel,
        jax.ShapeDtypeStruct((rows, size, width), BF16),
        [SMEM, SMEM, VMEM, VMEM],
        VMEM,
        flops=work * (rows - 2),
        moved=read * (rows - 2),
    )(table, slots, adjacency, pool_two)
    out = call(
        place_kernel,
        jax.ShapeDtypeStruct((rows, size, width), BF16),
        [SMEM, VMEM, ANY],
        ANY,
        [pltpu.SemaphoreType.DMA((2,))],
        moved=4 * size * width * 2,
        input_output_aliases={2: 0},
    )(slots, moved, out)
    return out.reshape(rows * size, width)


def solution(mesh):
    in_specs = (P("dom", "feat"), P("dom", None, None, None), P(), P(), P(), P())
    return jax.shard_map(
        on_device, mesh=mesh, in_specs=in_specs, out_specs=P("dom", "feat"), check_vma=False
    )
```

```python
import functools

import jax
import jax.numpy as jnp
from jax import lax
from jax.experimental import pallas as pl
from jax.experimental.pallas import tpu as pltpu
from jax.sharding import PartitionSpec as P


BF16 = jnp.bfloat16
F32 = jnp.float32
I32 = jnp.int32
VMEM = pl.BlockSpec(memory_space=pltpu.VMEM)
SMEM = pl.BlockSpec(memory_space=pltpu.SMEM)
ANY = pl.BlockSpec(memory_space=pl.ANY)
HBM = pl.BlockSpec(memory_space=pltpu.HBM)


def swap(value, axis, flip):
    return lax.ppermute(value, axis, [(i, i ^ flip) for i in range(lax.axis_size(axis))])


def block(shape, dtype=BF16):
    return pltpu.VMEM(shape, dtype)


def scalars(shape):
    return pltpu.SMEM(shape, I32)


def copy_all(*triples):
    copies = [pltpu.make_async_copy(*triple) for triple in triples]
    for copy in copies:
        copy.start()
    for copy in copies:
        copy.wait()


def load_kernel(tiles_ref, mig_ref, x_ref, named_ref, slots_ref, own_ref, pair_ref, sems):
    copy_all(
        (tiles_ref, named_ref, sems.at[0]),
        (mig_ref, slots_ref, sems.at[1]),
        (x_ref, own_ref, sems.at[2]),
    )
    me = lax.axis_index("dom")
    for m in range(2):
        pair_ref[m] = own_ref[slots_ref[m, me]]


def write_sends(domains, slots_ref, own_ref, near_refs, far_refs):
    half = domains // 2
    for k in range(1, half):
        near_refs[k - 1][0] = own_ref[slots_ref[2 * k]]
        near_refs[k - 1][1] = own_ref[slots_ref[2 * k + 1]]
    for k in range(half, domains):
        far_refs[k - half][0] = own_ref[slots_ref[2 * k + 1]]


def first_kernel(domains, rows, mig, tiles_ref, own_ref, slots_ref, which_ref, deal_ref, *sends):
    half = domains // 2
    me = lax.axis_index("dom")
    mine0, mine1 = mig[0, me], mig[1, me]
    slots_ref[0] = mine0
    slots_ref[1] = mine1
    deal_ref[0] = mine0
    deal_ref[1] = mine1
    place = jnp.int32(2)
    for s in range(rows):
        deal_ref[place] = s
        place = place + jnp.where((mine0 == s) | (mine1 == s), 0, 1)
    opposite = me ^ half
    opposite_last = opposite * rows + mig[1, opposite]

    named = tiles_ref[...]
    user = lax.broadcasted_iota(I32, named.shape, 1) // rows
    slot = named - me * rows
    leaves = (slot == mine0) | (slot == mine1)
    staying = jnp.where((slot >= 0) & (slot < rows) & jnp.logical_not(leaves), slot, 0)
    last = jnp.where(slot == mine1, 1, 0)
    relayed = jnp.where(named == opposite_last, 1, 0)

    def requests(k):
        asks = user == (me ^ k)
        slots_ref[2 * k + 1] = jnp.max(jnp.where(asks, staying, 0))
        slots_ref[2 * k] = jnp.where(jnp.max(jnp.where(asks, last, 0)) == 1, mine1, mine0)
        which_ref[k] = jnp.max(jnp.where(asks, relayed, 0))

    if domains <= 16:
        for k in range(1, domains):
            requests(k)
    else:
        pl.loop(1, domains)(requests)
    write_sends(domains, slots_ref, own_ref, sends[: half - 1], sends[half - 1 :])


def table_kernel(
    domains, rows, mig, tiles_ref, adjacency_ref, table_ref, held_ref, found_ref, sems
):
    load = pltpu.make_async_copy(adjacency_ref, held_ref, sems.at[0])
    load.start()
    half = domains // 2
    named = tiles_ref[...]
    user = lax.broadcasted_iota(I32, named.shape, 1) // rows
    holder = named // rows
    slot = named - holder * rows
    flip = holder ^ user

    def mark(q, carry):
        first, last = carry
        here = holder == q
        first = first | (here & (slot == mig[0, q])).astype(I32)
        last = last | (here & (slot == mig[1, q])).astype(I32)
        return first, last

    zeros = jnp.zeros_like(named)
    first, last = lax.fori_loop(0, domains, mark, (zeros, zeros))
    leaves = first | last
    place = rows + 2 * flip + 1 - leaves
    place = jnp.where((flip == half) & (leaves == 1), rows + last, place)
    found_ref[...] = jnp.where(flip == 0, slot, place)
    copy_all((found_ref, table_ref, sems.at[1]))
    load.wait()


def relay_kernel(half, which_ref, pair_ref, *outs):
    for k in range(1, half):
        outs[k - 1][0] = pair_ref[which_ref[k]]


def fill_early_kernel(domains, own_ref, *refs):
    *arrived, pool_ref = refs
    half = domains // 2
    rows = own_ref.shape[0]
    pool_ref[0:rows] = own_ref[...]
    pool_ref[rows : rows + 2] = arrived[0][...]
    for k in range(1, half):
        pool_ref[rows + 2 * k : rows + 2 * k + 2] = arrived[k][...]
    pool_ref[rows + 2 * half + 1] = arrived[half][0]
    for k in range(half + 2, domains):
        pool_ref[rows + 2 * k + 1] = arrived[k - 1][0]


def fill_late(domains, rows, late, pool_ref):
    half = domains // 2
    pool_ref[rows + 2 * (half + 1) + 1] = late[0][0]
    for k in range(1, half):
        pool_ref[rows + 2 * (half + k)] = late[k][0]


def sum_row(r, table_ref, adjacency_ref, pool_ref):
    rows, tiles = adjacency_ref.shape[:2]
    g = lax.axis_index("dom") * rows + r
    total = None
    for t in range(0, tiles, 2):
        left = jnp.concatenate([adjacency_ref[r, t], adjacency_ref[r, t + 1]], axis=1)
        right = jnp.concatenate(
            [pool_ref[table_ref[t, g]], pool_ref[table_ref[t + 1, g]]], axis=0
        )
        part = jnp.dot(left, right, preferred_element_type=F32)
        total = part if total is None else total + part
    return total.astype(BF16)


def first_sum_kernel(domains, feats, j, table_ref, deal_ref, adjacency_ref, *refs):
    _, *late, pool_ref, out_ref = refs
    fill_late(domains, adjacency_ref.shape[0], late, pool_ref)
    part_sum_kernel(feats, [j], table_ref, deal_ref, adjacency_ref, pool_ref, out_ref)


def part_sum_kernel(feats, js, table_ref, deal_ref, adjacency_ref, pool_ref, *outs):
    for j, out_ref in zip(js, outs, strict=True):
        rank = lax.axis_index("feat") ^ j

        @pl.loop(0, out_ref.shape[0])
        def _(i, rank=rank, out_ref=out_ref):
            out_ref[i] = sum_row(deal_ref[i * feats + rank], table_ref, adjacency_ref, pool_ref)


def leaving_sum_kernel(domains, table_ref, slots_ref, adjacency_ref, *refs):
    _, *late, pool_ref, out_ref = refs
    fill_late(domains, adjacency_ref.shape[0], late, pool_ref)

    @pl.loop(0, out_ref.shape[0])
    def _(i):
        out_ref[i] = sum_row(slots_ref[i], table_ref, adjacency_ref, pool_ref)


def staying_sum_kernel(table_ref, slots_ref, adjacency_ref, pool_ref, out_ref):
    @pl.loop(0, out_ref.shape[0])
    def _(r):
        @pl.when((r != slots_ref[0]) & (r != slots_ref[1]))
        def _():
            out_ref[r] = sum_row(r, table_ref, adjacency_ref, pool_ref)


def first_products(js, parts, chunk, weight_ref, c):
    feat = lax.axis_index("feat")
    width = parts[0].shape[2]
    total = None
    for j, part in zip(js, parts, strict=True):
        start = pl.multiple_of((feat ^ j) * width, width)
        weight = weight_ref[pl.ds(start, width), c : c + width]
        product = jnp.dot(part[chunk], weight, preferred_element_type=F32)
        total = product if total is None else total + product
    return total


def dense_early_kernel(weight_one_ref, *refs):
    *parts, total_ref = refs
    width = parts[0].shape[2]
    for chunk in range(total_ref.shape[0]):
        for c in range(0, weight_one_ref.shape[1], width):
            total_ref[chunk, :, c : c + width] = first_products(
                range(2), parts, chunk, weight_one_ref, c
            )


def dense_kernel(feats, chunk, weight_one_ref, weight_two_ref, total_ref, *refs):
    n_parts = feats - 2
    parts, outs, hidden_ref = refs[:n_parts], refs[n_parts:-1], refs[-1]
    feat = lax.axis_index("feat")
    width = parts[0].shape[2]
    for c in range(0, weight_one_ref.shape[1], width):
        late = first_products(range(2, feats), parts, chunk, weight_one_ref, c)
        total = total_ref[chunk, :, c : c + width] + late
        hidden_ref[:, c : c + width] = jnp.maximum(total, 0.0).astype(BF16)
    for j in range(feats):
        start = pl.multiple_of((feat ^ j) * width, width)
        outs[j][0] = jnp.dot(
            hidden_ref[...],
            weight_two_ref[:, pl.ds(start, width)],
            preferred_element_type=F32,
        ).astype(BF16)


def second_pair_kernel(*refs):
    *blocks, pair_ref = refs
    feat = lax.axis_index("feat")
    for j, ref in enumerate(blocks):

        @pl.when((feat ^ j) < 2)
        def _(j=j, ref=ref):
            pair_ref[feat ^ j] = ref[0]


def second_kernel(domains, feats, slots_ref, deal_ref, *refs):
    half = domains // 2
    n_blocks = len(refs) - 1 - (domains - 1)
    blocks, own_ref, sends = refs[:n_blocks], refs[n_blocks], refs[n_blocks + 1 :]
    feat = lax.axis_index("feat")
    for n, ref in enumerate(blocks):
        i, j = divmod(n, feats)
        own_ref[deal_ref[i * feats + (feat ^ j)]] = ref[0]
    write_sends(domains, slots_ref, own_ref, sends[: half - 1], sends[half - 1 :])


def place_kernel(slots_ref, moved_ref, out_in_ref, out_ref, sems):
    del out_in_ref
    copies = [
        pltpu.make_async_copy(moved_ref.at[i], out_ref.at[slots_ref[i]], sems.at[i])
        for i in range(moved_ref.shape[0])
    ]
    for copy in copies:
        copy.start()
    for copy in copies:
        copy.wait()


def call(body, out_shape, in_specs, out_specs, scratch=(), flops=0, moved=0, **kwargs):
    run = pl.pallas_call(
        body,
        out_shape=out_shape,
        in_specs=in_specs,
        out_specs=out_specs,
        scratch_shapes=list(scratch),
        cost_estimate=pl.CostEstimate(flops=flops, bytes_accessed=moved, transcendentals=0),
        compiler_params=pltpu.CompilerParams(vmem_limit_bytes=16 << 20),
        **kwargs,
    )

    def place_and_run(*args):
        placed = [
            a if spec is ANY else pltpu.with_memory_space_constraint(a, spec.memory_space)
            for a, spec in zip(args, in_specs, strict=True)
        ]
        return run(*placed)

    return place_and_run


def exchange(domains, own, pair, sends, which):
    half = domains // 2
    shape = pair.shape[1:]
    near, far = sends[: half - 1], sends[half - 1 :]
    pair = swap(pair, "dom", half)
    near = [swap(near[k - 1], "dom", k) for k in range(1, half)]
    far = [swap(far[k - half], "dom", k) for k in range(half, domains)]
    relay = call(
        functools.partial(relay_kernel, half),
        [block((1, *shape))] * (half - 1),
        [SMEM, VMEM],
        [VMEM] * (half - 1),
        moved=4 * pair.size * half,
    )(which, pair)
    relay = [swap(relay[k - 1], "dom", k) for k in range(1, half)]
    early = [pair, *near, far[0], *far[2:]]
    pool = call(
        functools.partial(fill_early_kernel, domains),
        [block((own.shape[0] + 2 * domains, *shape))],
        [VMEM] * (1 + len(early)),
        [VMEM],
        moved=8 * own.size,
    )(own, *early)[0]
    return [pool, far[1], *relay]


def on_device(features, adjacency, tile_src, mig_slot, weight_one, weight_two):
    domains = lax.axis_size("dom")
    feats = lax.axis_size("feat")
    half = domains // 2
    rows, tiles, size, _ = adjacency.shape
    width = features.shape[1]
    per = rows // feats
    blocks = features.reshape(rows, size, width)
    named, leaving_slots = tile_src.T, mig_slot.T
    near_far = [block((2, size, width))] * (half - 1) + [block((1, size, width))] * half
    pool = block((rows + 2 * domains, size, width))
    work = 2 * tiles * size * size * width
    read = adjacency.size * 2 // rows
    named, mig, own, pair = call(
        load_kernel,
        [
            block(named.shape, I32),
            scalars(leaving_slots.shape),
            block((rows, size, width)),
            block((2, size, width)),
        ],
        [HBM, HBM, HBM],
        [VMEM, SMEM, VMEM, VMEM],
        [pltpu.SemaphoreType.DMA((3,))],
        moved=features.size * 2,
    )(named, leaving_slots, blocks)
    slots, which, deal, *sends = call(
        functools.partial(first_kernel, domains, rows),
        [scalars((2 * domains,)), scalars((domains,)), scalars((rows + 1,)), *near_far],
        [SMEM, VMEM, VMEM],
        [SMEM] * 3 + [VMEM] * len(near_far),
        moved=8 * size * width * domains,
    )(mig, named, own)
    arrived = exchange(domains, own, pair, sends, which)
    table, adjacency = call(
        functools.partial(table_kernel, domains, rows),
        [scalars(named.shape), block(adjacency.shape)],
        [SMEM, VMEM, HBM],
        [SMEM, VMEM],
        [pltpu.VMEM(named.shape, I32), pltpu.SemaphoreType.DMA((2,))],
        moved=adjacency.size * 2,
    )(mig, named, adjacency)

    one = block((1, size, width))
    whole = block((per, size, width))
    parts = [None] * feats
    pool_one, parts[2] = call(
        functools.partial(first_sum_kernel, domains, feats, 2),
        [pool, whole],
        [SMEM, SMEM] + [VMEM] * (1 + len(arrived)),
        [VMEM] * 2,
        flops=work * per,
        moved=read * per,
        input_output_aliases={3: 0},
    )(table, deal, adjacency, *arrived)
    for js in [[j] for j in range(3, feats)] + [[1, 0]]:
        outs = call(
            functools.partial(part_sum_kernel, feats, js),
            [whole] * len(js),
            [SMEM, SMEM, VMEM, VMEM],
            [VMEM] * len(js),
            flops=work * per * len(js),
            moved=read * per * len(js),
        )(table, deal, adjacency, pool_one)
        for j, out in zip(js, outs):
            parts[j] = out
    parts = [p if j == 0 else swap(p, "feat", j) for j, p in enumerate(parts)]

    total = call(
        dense_early_kernel,
        [pltpu.VMEM((per, size, weight_one.shape[1]), F32)],
        [VMEM] * 3,
        [VMEM],
        flops=2 * per * size * weight_one.size * 2 // feats,
        moved=weight_one.size * 2,
    )(weight_one, *parts[:2])[0]
    columns = []
    for i in range(per):
        outs = call(
            functools.partial(dense_kernel, feats, i),
            [one] * feats,
            [VMEM] * (1 + feats),
            [VMEM] * feats,
            [pltpu.VMEM((size, weight_one.shape[1]), BF16)],
            flops=4 * size * weight_one.size,
            moved=weight_one.size * 4,
        )(weight_one, weight_two, total, *parts[2:])
        columns += [c if j == 0 else swap(c, "feat", j) for j, c in enumerate(outs)]

    pair = call(
        second_pair_kernel,
        [block((2, size, width))],
        [VMEM] * feats,
        [VMEM],
        moved=8 * size * width,
    )(*columns[:feats])[0]
    own, *sends = call(
        functools.partial(second_kernel, domains, feats),
        [block((rows, size, width)), *near_far],
        [SMEM, SMEM] + [VMEM] * len(columns),
        [VMEM] * (1 + len(near_far)),
        moved=8 * size * width * domains,
    )(slots, deal, *columns)
    arrived = exchange(domains, own, pair, sends, which)

    pool_two, leaving = call(
        functools.partial(leaving_sum_kernel, domains),
        [pool, block((2, size, width))],
        [SMEM, SMEM] + [VMEM] * (1 + len(arrived)),
        [VMEM] * 2,
        flops=work * 2,
        moved=read * 2,
        input_output_aliases={3: 0},
    )(table, slots, adjacency, *arrived)
    moved = lax.ppermute(leaving, "dom", [(i, (i + 1) % domains) for i in range(domains)])
    out = call(
        staying_sum_kernel,
        jax.ShapeDtypeStruct((rows, size, width), BF16),
        [SMEM, SMEM, VMEM, VMEM],
        VMEM,
        flops=work * (rows - 2),
        moved=read * (rows - 2),
    )(table, slots, adjacency, pool_two)
    out = call(
        place_kernel,
        jax.ShapeDtypeStruct((rows, size, width), BF16),
        [SMEM, VMEM, ANY],
        ANY,
        [pltpu.SemaphoreType.DMA((2,))],
        moved=4 * size * width * 2,
        input_output_aliases={2: 0},
    )(slots, moved, out)
    return out.reshape(rows * size, width)


def solution(mesh):
    in_specs = (P("dom", "feat"), P("dom", None, None, None), P(), P(), P(), P())
    return jax.shard_map(
        on_device, mesh=mesh, in_specs=in_specs, out_specs=P("dom", "feat"), check_vma=False
    )
```

```python
import functools

import jax
import jax.numpy as jnp
from jax import lax
from jax.experimental import pallas as pl
from jax.experimental.pallas import tpu as pltpu
from jax.sharding import PartitionSpec as P


BF16 = jnp.bfloat16
F32 = jnp.float32
I32 = jnp.int32
VMEM = pl.BlockSpec(memory_space=pltpu.VMEM)
SMEM = pl.BlockSpec(memory_space=pltpu.SMEM)
ANY = pl.BlockSpec(memory_space=pl.ANY)
HBM = pl.BlockSpec(memory_space=pltpu.HBM)


def swap(value, axis, flip):
    return lax.ppermute(value, axis, [(i, i ^ flip) for i in range(lax.axis_size(axis))])


def block(shape, dtype=BF16):
    return pltpu.VMEM(shape, dtype)


def scalars(shape):
    return pltpu.SMEM(shape, I32)


def copy_all(*triples):
    copies = [pltpu.make_async_copy(*triple) for triple in triples]
    for copy in copies:
        copy.start()
    for copy in copies:
        copy.wait()


def load_kernel(tiles_ref, mig_ref, x_ref, named_ref, slots_ref, own_ref, pair_ref, sems):
    copy_all(
        (tiles_ref, named_ref, sems.at[0]),
        (mig_ref, slots_ref, sems.at[1]),
        (x_ref, own_ref, sems.at[2]),
    )
    me = lax.axis_index("dom")
    for m in range(2):
        pair_ref[m] = own_ref[slots_ref[m, me]]


def write_sends(domains, slots_ref, own_ref, near_refs, far_refs):
    half = domains // 2
    for k in range(1, half):
        near_refs[k - 1][0] = own_ref[slots_ref[2 * k]]
        near_refs[k - 1][1] = own_ref[slots_ref[2 * k + 1]]
    for k in range(half, domains):
        far_refs[k - half][0] = own_ref[slots_ref[2 * k + 1]]


def first_kernel(domains, rows, mig, tiles_ref, own_ref, slots_ref, which_ref, deal_ref, *sends):
    half = domains // 2
    me = lax.axis_index("dom")
    mine0, mine1 = mig[0, me], mig[1, me]
    slots_ref[0] = mine0
    slots_ref[1] = mine1
    deal_ref[0] = mine0
    deal_ref[1] = mine1
    place = jnp.int32(2)
    for s in range(rows):
        deal_ref[place] = s
        place = place + jnp.where((mine0 == s) | (mine1 == s), 0, 1)
    opposite = me ^ half
    opposite_last = opposite * rows + mig[1, opposite]

    named = tiles_ref[...]
    user = lax.broadcasted_iota(I32, named.shape, 1) // rows
    slot = named - me * rows
    leaves = (slot == mine0) | (slot == mine1)
    staying = jnp.where((slot >= 0) & (slot < rows) & jnp.logical_not(leaves), slot, 0)
    last = jnp.where(slot == mine1, 1, 0)
    relayed = jnp.where(named == opposite_last, 1, 0)

    def requests(k):
        asks = user == (me ^ k)
        slots_ref[2 * k + 1] = jnp.max(jnp.where(asks, staying, 0))
        slots_ref[2 * k] = jnp.where(jnp.max(jnp.where(asks, last, 0)) == 1, mine1, mine0)
        which_ref[k] = jnp.max(jnp.where(asks, relayed, 0))

    if domains <= 16:
        for k in range(1, domains):
            requests(k)
    else:
        pl.loop(1, domains)(requests)
    write_sends(domains, slots_ref, own_ref, sends[: half - 1], sends[half - 1 :])


def table_kernel(domains, rows, mig, tiles_ref, *refs):
    sources, table_ref, targets, found_ref, sems = refs[:3], refs[3], refs[4:7], refs[7], refs[8]
    loads = [
        pltpu.make_async_copy(source, target, sems.at[n])
        for n, (source, target) in enumerate(zip(sources, targets))
    ]
    for load in loads:
        load.start()
    half = domains // 2
    named = tiles_ref[...]
    user = lax.broadcasted_iota(I32, named.shape, 1) // rows
    holder = named // rows
    slot = named - holder * rows
    flip = holder ^ user

    def mark(q, carry):
        first, last = carry
        here = holder == q
        first = first | (here & (slot == mig[0, q])).astype(I32)
        last = last | (here & (slot == mig[1, q])).astype(I32)
        return first, last

    zeros = jnp.zeros_like(named)
    first, last = lax.fori_loop(0, domains, mark, (zeros, zeros))
    leaves = first | last
    place = rows + 2 * flip + 1 - leaves
    place = jnp.where((flip == half) & (leaves == 1), rows + last, place)
    found_ref[...] = jnp.where(flip == 0, slot, place)
    copy_all((found_ref, table_ref, sems.at[3]))
    for load in loads:
        load.wait()


def relay_kernel(half, which_ref, pair_ref, *outs):
    for k in range(1, half):
        outs[k - 1][0] = pair_ref[which_ref[k]]


def fill_early_kernel(domains, own_ref, *refs):
    *arrived, pool_ref = refs
    half = domains // 2
    rows = own_ref.shape[0]
    pool_ref[0:rows] = own_ref[...]
    pool_ref[rows : rows + 2] = arrived[0][...]
    for k in range(1, half):
        pool_ref[rows + 2 * k : rows + 2 * k + 2] = arrived[k][...]
    pool_ref[rows + 2 * half + 1] = arrived[half][0]
    for k in range(half + 2, domains):
        pool_ref[rows + 2 * k + 1] = arrived[k - 1][0]


def fill_late(domains, rows, late, pool_ref):
    half = domains // 2
    pool_ref[rows + 2 * (half + 1) + 1] = late[0][0]
    for k in range(1, half):
        pool_ref[rows + 2 * (half + k)] = late[k][0]


def sum_row(r, table_ref, adjacency_ref, pool_ref):
    rows, tiles = adjacency_ref.shape[:2]
    g = lax.axis_index("dom") * rows + r
    total = None
    for t in range(0, tiles, 2):
        left = jnp.concatenate([adjacency_ref[r, t], adjacency_ref[r, t + 1]], axis=1)
        right = jnp.concatenate(
            [pool_ref[table_ref[t, g]], pool_ref[table_ref[t + 1, g]]], axis=0
        )
        part = jnp.dot(left, right, preferred_element_type=F32)
        total = part if total is None else total + part
    return total.astype(BF16)


def first_sum_kernel(domains, feats, part, table_ref, deal_ref, adjacency_ref, *refs):
    _, *late, pool_ref, out_ref = refs
    fill_late(domains, adjacency_ref.shape[0], late, pool_ref)
    part_sum_kernel(feats, [part], table_ref, deal_ref, adjacency_ref, pool_ref, out_ref)


def part_sum_kernel(feats, parts, table_ref, deal_ref, adjacency_ref, pool_ref, *outs):
    for (i, j), out_ref in zip(parts, outs, strict=True):
        row = deal_ref[i * feats + (lax.axis_index("feat") ^ j)]
        out_ref[0] = sum_row(row, table_ref, adjacency_ref, pool_ref)


def leaving_sum_kernel(domains, table_ref, slots_ref, adjacency_ref, *refs):
    _, *late, pool_ref, out_ref = refs
    fill_late(domains, adjacency_ref.shape[0], late, pool_ref)

    @pl.loop(0, out_ref.shape[0])
    def _(i):
        out_ref[i] = sum_row(slots_ref[i], table_ref, adjacency_ref, pool_ref)


def staying_sum_kernel(table_ref, slots_ref, adjacency_ref, pool_ref, out_ref):
    @pl.loop(0, out_ref.shape[0])
    def _(r):
        @pl.when((r != slots_ref[0]) & (r != slots_ref[1]))
        def _():
            out_ref[r] = sum_row(r, table_ref, adjacency_ref, pool_ref)


def dense_kernel(feats, weight_one_ref, weight_two_ref, *refs):
    parts, outs, hidden_ref = refs[:feats], refs[feats : 2 * feats], refs[2 * feats]
    feat = lax.axis_index("feat")
    width = parts[0].shape[2]
    columns = weight_one_ref.shape[1]
    rows = [part[0] for part in parts]
    for c in range(0, columns, width):
        total = None
        for j in range(feats):
            start = pl.multiple_of((feat ^ j) * width, width)
            part = jnp.dot(
                rows[j],
                weight_one_ref[pl.ds(start, width), c : c + width],
                preferred_element_type=F32,
            )
            total = part if total is None else total + part
        hidden_ref[:, c : c + width] = jnp.maximum(total, 0.0).astype(BF16)
    for j in range(feats):
        start = pl.multiple_of((feat ^ j) * width, width)
        outs[j][0] = jnp.dot(
            hidden_ref[...],
            weight_two_ref[:, pl.ds(start, width)],
            preferred_element_type=F32,
        ).astype(BF16)


def second_pair_kernel(*refs):
    *blocks, pair_ref = refs
    feat = lax.axis_index("feat")
    for j, ref in enumerate(blocks):

        @pl.when((feat ^ j) < 2)
        def _(j=j, ref=ref):
            pair_ref[feat ^ j] = ref[0]


def second_kernel(domains, feats, slots_ref, deal_ref, *refs):
    half = domains // 2
    n_blocks = len(refs) - 1 - (domains - 1)
    blocks, own_ref, sends = refs[:n_blocks], refs[n_blocks], refs[n_blocks + 1 :]
    feat = lax.axis_index("feat")
    for n, ref in enumerate(blocks):
        i, j = divmod(n, feats)
        own_ref[deal_ref[i * feats + (feat ^ j)]] = ref[0]
    write_sends(domains, slots_ref, own_ref, sends[: half - 1], sends[half - 1 :])


def place_kernel(slots_ref, moved_ref, out_in_ref, out_ref, sems):
    del out_in_ref
    copies = [
        pltpu.make_async_copy(moved_ref.at[i], out_ref.at[slots_ref[i]], sems.at[i])
        for i in range(moved_ref.shape[0])
    ]
    for copy in copies:
        copy.start()
    for copy in copies:
        copy.wait()


def call(body, out_shape, in_specs, out_specs, scratch=(), flops=0, moved=0, **kwargs):
    run = pl.pallas_call(
        body,
        out_shape=out_shape,
        in_specs=in_specs,
        out_specs=out_specs,
        scratch_shapes=list(scratch),
        cost_estimate=pl.CostEstimate(flops=flops, bytes_accessed=moved, transcendentals=0),
        compiler_params=pltpu.CompilerParams(vmem_limit_bytes=16 << 20),
        **kwargs,
    )

    def place_and_run(*args):
        placed = [
            a if spec is ANY else pltpu.with_memory_space_constraint(a, spec.memory_space)
            for a, spec in zip(args, in_specs, strict=True)
        ]
        return run(*placed)

    return place_and_run


def exchange(domains, own, pair, sends, which):
    half = domains // 2
    shape = pair.shape[1:]
    near, far = sends[: half - 1], sends[half - 1 :]
    pair = swap(pair, "dom", half)
    near = [swap(near[k - 1], "dom", k) for k in range(1, half)]
    far = [swap(far[k - half], "dom", k) for k in range(half, domains)]
    relay = call(
        functools.partial(relay_kernel, half),
        [block((1, *shape))] * (half - 1),
        [SMEM, VMEM],
        [VMEM] * (half - 1),
        moved=4 * pair.size * half,
    )(which, pair)
    relay = [swap(relay[k - 1], "dom", k) for k in range(1, half)]
    early = [pair, *near, far[0], *far[2:]]
    pool = call(
        functools.partial(fill_early_kernel, domains),
        [block((own.shape[0] + 2 * domains, *shape))],
        [VMEM] * (1 + len(early)),
        [VMEM],
        moved=8 * own.size,
    )(own, *early)[0]
    return [pool, far[1], *relay]


def on_device(features, adjacency, tile_src, mig_slot, weight_one, weight_two):
    domains = lax.axis_size("dom")
    feats = lax.axis_size("feat")
    half = domains // 2
    rows, tiles, size, _ = adjacency.shape
    width = features.shape[1]
    per = rows // feats
    blocks = features.reshape(rows, size, width)
    named, leaving_slots = tile_src.T, mig_slot.T
    near_far = [block((2, size, width))] * (half - 1) + [block((1, size, width))] * half
    pool = block((rows + 2 * domains, size, width))
    work = 2 * tiles * size * size * width
    read = adjacency.size * 2 // rows
    named, mig, own, pair = call(
        load_kernel,
        [
            block(named.shape, I32),
            scalars(leaving_slots.shape),
            block((rows, size, width)),
            block((2, size, width)),
        ],
        [HBM, HBM, HBM],
        [VMEM, SMEM, VMEM, VMEM],
        [pltpu.SemaphoreType.DMA((3,))],
        moved=features.size * 2,
    )(named, leaving_slots, blocks)
    slots, which, deal, *sends = call(
        functools.partial(first_kernel, domains, rows),
        [scalars((2 * domains,)), scalars((domains,)), scalars((rows + 1,)), *near_far],
        [SMEM, VMEM, VMEM],
        [SMEM] * 3 + [VMEM] * len(near_far),
        moved=8 * size * width * domains,
    )(mig, named, own)
    arrived = exchange(domains, own, pair, sends, which)
    loaded = (adjacency, weight_one, weight_two)
    table, adjacency, weight_one, weight_two = call(
        functools.partial(table_kernel, domains, rows),
        [scalars(named.shape)] + [block(x.shape) for x in loaded],
        [SMEM, VMEM, HBM, HBM, HBM],
        [SMEM, VMEM, VMEM, VMEM],
        [pltpu.VMEM(named.shape, I32), pltpu.SemaphoreType.DMA((4,))],
        moved=sum(x.size for x in loaded) * 2,
    )(mig, named, *loaded)

    one = block((1, size, width))
    crossing = [(i, j) for i in range(per) for j in range(2, feats)]
    parts = {}
    pool_one, parts[crossing[0]] = call(
        functools.partial(first_sum_kernel, domains, feats, crossing[0]),
        [pool, one],
        [SMEM, SMEM] + [VMEM] * (1 + len(arrived)),
        [VMEM] * 2,
        flops=work,
        moved=read,
        input_output_aliases={3: 0},
    )(table, deal, adjacency, *arrived)
    for group in [[part] for part in crossing[1:]] + [[(i, 1), (i, 0)] for i in range(per)]:
        outs = call(
            functools.partial(part_sum_kernel, feats, group),
            [one] * len(group),
            [SMEM, SMEM, VMEM, VMEM],
            [VMEM] * len(group),
            flops=work * len(group),
            moved=read * len(group),
        )(table, deal, adjacency, pool_one)
        parts.update(zip(group, outs))
    parts = {(i, j): p if j == 0 else swap(p, "feat", j) for (i, j), p in parts.items()}
    columns = []
    for i in range(per):
        outs = call(
            functools.partial(dense_kernel, feats),
            [one] * feats,
            [VMEM] * (2 + feats),
            [VMEM] * feats,
            [pltpu.VMEM((size, weight_one.shape[1]), BF16)],
            flops=4 * size * weight_one.size,
            moved=weight_one.size * 4,
        )(weight_one, weight_two, *[parts[i, j] for j in range(feats)])
        columns += [c if j == 0 else swap(c, "feat", j) for j, c in enumerate(outs)]

    pair = call(
        second_pair_kernel,
        [block((2, size, width))],
        [VMEM] * feats,
        [VMEM],
        moved=8 * size * width,
    )(*columns[:feats])[0]
    own, *sends = call(
        functools.partial(second_kernel, domains, feats),
        [block((rows, size, width)), *near_far],
        [SMEM, SMEM] + [VMEM] * len(columns),
        [VMEM] * (1 + len(near_far)),
        moved=8 * size * width * domains,
    )(slots, deal, *columns)
    arrived = exchange(domains, own, pair, sends, which)

    pool_two, leaving = call(
        functools.partial(leaving_sum_kernel, domains),
        [pool, block((2, size, width))],
        [SMEM, SMEM] + [VMEM] * (1 + len(arrived)),
        [VMEM] * 2,
        flops=work * 2,
        moved=read * 2,
        input_output_aliases={3: 0},
    )(table, slots, adjacency, *arrived)
    moved = lax.ppermute(leaving, "dom", [(i, (i + 1) % domains) for i in range(domains)])
    out = call(
        staying_sum_kernel,
        jax.ShapeDtypeStruct((rows, size, width), BF16),
        [SMEM, SMEM, VMEM, VMEM],
        VMEM,
        flops=work * (rows - 2),
        moved=read * (rows - 2),
    )(table, slots, adjacency, pool_two)
    out = call(
        place_kernel,
        jax.ShapeDtypeStruct((rows, size, width), BF16),
        [SMEM, VMEM, ANY],
        ANY,
        [pltpu.SemaphoreType.DMA((2,))],
        moved=4 * size * width * 2,
        input_output_aliases={2: 0},
    )(slots, moved, out)
    return out.reshape(rows * size, width)


def solution(mesh):
    in_specs = (P("dom", "feat"), P("dom", None, None, None), P(), P(), P(), P())
    return jax.shard_map(
        on_device, mesh=mesh, in_specs=in_specs, out_specs=P("dom", "feat"), check_vma=False
    )
```

```python
import functools

import jax
import jax.numpy as jnp
from jax import lax
from jax.experimental import pallas as pl
from jax.experimental.pallas import tpu as pltpu
from jax.sharding import PartitionSpec as P


BF16 = jnp.bfloat16
F32 = jnp.float32
I32 = jnp.int32
VMEM = pl.BlockSpec(memory_space=pltpu.VMEM)
SMEM = pl.BlockSpec(memory_space=pltpu.SMEM)
ANY = pl.BlockSpec(memory_space=pl.ANY)
HBM = pl.BlockSpec(memory_space=pltpu.HBM)


def swap(value, axis, flip):
    return lax.ppermute(value, axis, [(i, i ^ flip) for i in range(lax.axis_size(axis))])


def far_order(domains, name):
    half = domains // 2
    others = [*range(domains - 2, half, -1)]
    if name == "two":
        others.reverse()
    return [half, domains - 1, *others]


def block(shape, dtype=BF16):
    return pltpu.VMEM(shape, dtype)


def scalars(shape):
    return pltpu.SMEM(shape, I32)


def copy_all(*triples):
    copies = [pltpu.make_async_copy(*triple) for triple in triples]
    for copy in copies:
        copy.start()
    for copy in copies:
        copy.wait()


def load_kernel(tiles_ref, mig_ref, x_ref, named_ref, slots_ref, own_ref, pair_ref, sems):
    copy_all(
        (tiles_ref, named_ref, sems.at[0]),
        (mig_ref, slots_ref, sems.at[1]),
        (x_ref, own_ref, sems.at[2]),
    )
    me = lax.axis_index("dom")
    for m in range(2):
        pair_ref[m] = own_ref[slots_ref[m, me]]


def write_sends(domains, slots_ref, own_ref, near_refs, far_refs):
    half = domains // 2
    for k in range(1, half):
        near_refs[k - 1][0] = own_ref[slots_ref[2 * k]]
        near_refs[k - 1][1] = own_ref[slots_ref[2 * k + 1]]
    for k in range(half, domains):
        far_refs[k - half][0] = own_ref[slots_ref[2 * k + 1]]


def first_kernel(domains, rows, mig, tiles_ref, own_ref, slots_ref, which_ref, deal_ref, *sends):
    half = domains // 2
    me = lax.axis_index("dom")
    mine0, mine1 = mig[0, me], mig[1, me]
    slots_ref[0] = mine0
    slots_ref[1] = mine1
    deal_ref[0] = mine0
    deal_ref[1] = mine1
    place = jnp.int32(2)
    for s in range(rows):
        deal_ref[place] = s
        place = place + jnp.where((mine0 == s) | (mine1 == s), 0, 1)
    opposite = me ^ half
    opposite_last = opposite * rows + mig[1, opposite]

    named = tiles_ref[...]
    user = lax.broadcasted_iota(I32, named.shape, 1) // rows
    slot = named - me * rows
    leaves = (slot == mine0) | (slot == mine1)
    staying = jnp.where((slot >= 0) & (slot < rows) & jnp.logical_not(leaves), slot, 0)
    last = jnp.where(slot == mine1, 1, 0)
    relayed = jnp.where(named == opposite_last, 1, 0)

    def requests(k):
        asks = user == (me ^ k)
        slots_ref[2 * k + 1] = jnp.max(jnp.where(asks, staying, 0))
        slots_ref[2 * k] = jnp.where(jnp.max(jnp.where(asks, last, 0)) == 1, mine1, mine0)
        which_ref[k] = jnp.max(jnp.where(asks, relayed, 0))

    if domains <= 16:
        for k in range(1, domains):
            requests(k)
    else:
        pl.loop(1, domains)(requests)
    write_sends(domains, slots_ref, own_ref, sends[: half - 1], sends[half - 1 :])


def table_kernel(domains, rows, mig, tiles_ref, *refs):
    sources, table_ref, targets, found_ref, sems = refs[:3], refs[3], refs[4:7], refs[7], refs[8]
    loads = [
        pltpu.make_async_copy(source, target, sems.at[n])
        for n, (source, target) in enumerate(zip(sources, targets))
    ]
    for load in loads:
        load.start()
    half = domains // 2
    named = tiles_ref[...]
    user = lax.broadcasted_iota(I32, named.shape, 1) // rows
    holder = named // rows
    slot = named - holder * rows
    flip = holder ^ user

    def mark(q, carry):
        first, last = carry
        here = holder == q
        first = first | (here & (slot == mig[0, q])).astype(I32)
        last = last | (here & (slot == mig[1, q])).astype(I32)
        return first, last

    zeros = jnp.zeros_like(named)
    first, last = lax.fori_loop(0, domains, mark, (zeros, zeros))
    leaves = first | last
    place = rows + 2 * flip + 1 - leaves
    place = jnp.where((flip == half) & (leaves == 1), rows + last, place)
    found_ref[...] = jnp.where(flip == 0, slot, place)
    copy_all((found_ref, table_ref, sems.at[3]))
    for load in loads:
        load.wait()


def relay_kernel(half, which_ref, pair_ref, *outs):
    for k in range(1, half):
        outs[k - 1][0] = pair_ref[which_ref[k]]


def fill_early_kernel(domains, name, own_ref, *refs):
    *arrived, pool_ref = refs
    half = domains // 2
    rows = own_ref.shape[0]
    pool_ref[0:rows] = own_ref[...]
    pool_ref[rows : rows + 2] = arrived[0][...]
    for k in range(1, half):
        pool_ref[rows + 2 * k : rows + 2 * k + 2] = arrived[k][...]
    for k, ref in zip(far_order(domains, name)[:-1], arrived[half:], strict=True):
        pool_ref[rows + 2 * k + 1] = ref[0]


def fill_late(domains, name, rows, late, pool_ref):
    half = domains // 2
    pool_ref[rows + 2 * far_order(domains, name)[-1] + 1] = late[0][0]
    for k in range(1, half):
        pool_ref[rows + 2 * (half + k)] = late[k][0]


def sum_row(r, table_ref, adjacency_ref, pool_ref):
    rows, tiles = adjacency_ref.shape[:2]
    g = lax.axis_index("dom") * rows + r
    total = None
    for t in range(0, tiles, 2):
        left = jnp.concatenate([adjacency_ref[r, t], adjacency_ref[r, t + 1]], axis=1)
        right = jnp.concatenate(
            [pool_ref[table_ref[t, g]], pool_ref[table_ref[t + 1, g]]], axis=0
        )
        part = jnp.dot(left, right, preferred_element_type=F32)
        total = part if total is None else total + part
    return total.astype(BF16)


def first_sum_kernel(domains, feats, part, table_ref, deal_ref, adjacency_ref, *refs):
    _, *late, pool_ref, out_ref = refs
    fill_late(domains, "one", adjacency_ref.shape[0], late, pool_ref)
    part_sum_kernel(feats, [part], table_ref, deal_ref, adjacency_ref, pool_ref, out_ref)


def part_sum_kernel(feats, parts, table_ref, deal_ref, adjacency_ref, pool_ref, *outs):
    for (i, j), out_ref in zip(parts, outs, strict=True):
        row = deal_ref[i * feats + (lax.axis_index("feat") ^ j)]
        out_ref[0] = sum_row(row, table_ref, adjacency_ref, pool_ref)


def leaving_sum_kernel(domains, table_ref, slots_ref, adjacency_ref, *refs):
    _, *late, pool_ref, out_ref = refs
    fill_late(domains, "two", adjacency_ref.shape[0], late, pool_ref)

    for i in range(out_ref.shape[0]):
        out_ref[i] = sum_row(slots_ref[i], table_ref, adjacency_ref, pool_ref)


def staying_sum_kernel(table_ref, slots_ref, adjacency_ref, pool_ref, out_ref):
    @pl.loop(0, out_ref.shape[0])
    def _(r):
        @pl.when((r != slots_ref[0]) & (r != slots_ref[1]))
        def _():
            out_ref[r] = sum_row(r, table_ref, adjacency_ref, pool_ref)


def dense_kernel(feats, weight_one_ref, weight_two_ref, *refs):
    parts, outs, hidden_ref = refs[:feats], refs[feats : 2 * feats], refs[2 * feats]
    feat = lax.axis_index("feat")
    width = parts[0].shape[2]
    columns = weight_one_ref.shape[1]
    rows = [part[0] for part in parts]
    for c in range(0, columns, width):
        total = None
        for j in range(feats):
            start = pl.multiple_of((feat ^ j) * width, width)
            part = jnp.dot(
                rows[j],
                weight_one_ref[pl.ds(start, width), c : c + width],
                preferred_element_type=F32,
            )
            total = part if total is None else total + part
        hidden_ref[:, c : c + width] = jnp.maximum(total, 0.0).astype(BF16)
    for j in range(feats):
        start = pl.multiple_of((feat ^ j) * width, width)
        outs[j][0] = jnp.dot(
            hidden_ref[...],
            weight_two_ref[:, pl.ds(start, width)],
            preferred_element_type=F32,
        ).astype(BF16)


def second_pair_kernel(*refs):
    *blocks, pair_ref = refs
    feat = lax.axis_index("feat")
    for j, ref in enumerate(blocks):

        @pl.when((feat ^ j) < 2)
        def _(j=j, ref=ref):
            pair_ref[feat ^ j] = ref[0]


def second_kernel(domains, feats, slots_ref, deal_ref, *refs):
    half = domains // 2
    n_blocks = len(refs) - 1 - (domains - 1)
    blocks, own_ref, sends = refs[:n_blocks], refs[n_blocks], refs[n_blocks + 1 :]
    feat = lax.axis_index("feat")
    for n, ref in enumerate(blocks):
        i, j = divmod(n, feats)
        own_ref[deal_ref[i * feats + (feat ^ j)]] = ref[0]
    write_sends(domains, slots_ref, own_ref, sends[: half - 1], sends[half - 1 :])


def place_kernel(slots_ref, moved_ref, out_in_ref, out_ref, sems):
    del out_in_ref
    copies = [
        pltpu.make_async_copy(moved_ref.at[i], out_ref.at[slots_ref[i]], sems.at[i])
        for i in range(moved_ref.shape[0])
    ]
    for copy in copies:
        copy.start()
    for copy in copies:
        copy.wait()


def call(body, out_shape, in_specs, out_specs, scratch=(), flops=0, moved=0, **kwargs):
    run = pl.pallas_call(
        body,
        out_shape=out_shape,
        in_specs=in_specs,
        out_specs=out_specs,
        scratch_shapes=list(scratch),
        cost_estimate=pl.CostEstimate(flops=flops, bytes_accessed=moved, transcendentals=0),
        compiler_params=pltpu.CompilerParams(vmem_limit_bytes=16 << 20),
        **kwargs,
    )

    def place_and_run(*args):
        placed = [
            a if spec is ANY else pltpu.with_memory_space_constraint(a, spec.memory_space)
            for a, spec in zip(args, in_specs, strict=True)
        ]
        return run(*placed)

    return place_and_run


def exchange(domains, own, pair, sends, which, name):
    half = domains // 2
    shape = pair.shape[1:]
    near, far = sends[: half - 1], sends[half - 1 :]
    pair = swap(pair, "dom", half)
    near = [swap(near[k - 1], "dom", k) for k in range(1, half)]
    far = [swap(far[k - half], "dom", k) for k in range(half, domains)]
    relay = call(
        functools.partial(relay_kernel, half),
        [block((1, *shape))] * (half - 1),
        [SMEM, VMEM],
        [VMEM] * (half - 1),
        moved=4 * pair.size * half,
    )(which, pair)
    relay = [swap(relay[k - 1], "dom", k) for k in range(1, half)]
    far = [far[k - half] for k in far_order(domains, name)]
    early = [pair, *near, *far[:-1]]
    pool = call(
        functools.partial(fill_early_kernel, domains, name),
        [block((own.shape[0] + 2 * domains, *shape))],
        [VMEM] * (1 + len(early)),
        [VMEM],
        moved=8 * own.size,
    )(own, *early)[0]
    return [pool, far[-1], *relay]


def on_device(features, adjacency, tile_src, mig_slot, weight_one, weight_two):
    domains = lax.axis_size("dom")
    feats = lax.axis_size("feat")
    half = domains // 2
    rows, tiles, size, _ = adjacency.shape
    width = features.shape[1]
    per = rows // feats
    blocks = features.reshape(rows, size, width)
    named, leaving_slots = tile_src.T, mig_slot.T
    near_far = [block((2, size, width))] * (half - 1) + [block((1, size, width))] * half
    pool = block((rows + 2 * domains, size, width))
    work = 2 * tiles * size * size * width
    read = adjacency.size * 2 // rows
    named, mig, own, pair = call(
        load_kernel,
        [
            block(named.shape, I32),
            scalars(leaving_slots.shape),
            block((rows, size, width)),
            block((2, size, width)),
        ],
        [HBM, HBM, HBM],
        [VMEM, SMEM, VMEM, VMEM],
        [pltpu.SemaphoreType.DMA((3,))],
        moved=features.size * 2,
    )(named, leaving_slots, blocks)
    slots, which, deal, *sends = call(
        functools.partial(first_kernel, domains, rows),
        [scalars((2 * domains,)), scalars((domains,)), scalars((rows + 1,)), *near_far],
        [SMEM, VMEM, VMEM],
        [SMEM] * 3 + [VMEM] * len(near_far),
        moved=8 * size * width * domains,
    )(mig, named, own)
    arrived = exchange(domains, own, pair, sends, which, "one")
    loaded = (adjacency, weight_one, weight_two)
    table, adjacency, weight_one, weight_two = call(
        functools.partial(table_kernel, domains, rows),
        [scalars(named.shape)] + [block(x.shape) for x in loaded],
        [SMEM, VMEM, HBM, HBM, HBM],
        [SMEM, VMEM, VMEM, VMEM],
        [pltpu.VMEM(named.shape, I32), pltpu.SemaphoreType.DMA((4,))],
        moved=sum(x.size for x in loaded) * 2,
    )(mig, named, *loaded)

    one = block((1, size, width))
    crossing = [(i, j) for i in range(per) for j in range(2, feats)]
    parts = {}
    pool_one, parts[crossing[0]] = call(
        functools.partial(first_sum_kernel, domains, feats, crossing[0]),
        [pool, one],
        [SMEM, SMEM] + [VMEM] * (1 + len(arrived)),
        [VMEM] * 2,
        flops=work,
        moved=read,
        input_output_aliases={3: 0},
    )(table, deal, adjacency, *arrived)
    for group in [[part] for part in crossing[1:]] + [[(i, 1), (i, 0)] for i in range(per)]:
        outs = call(
            functools.partial(part_sum_kernel, feats, group),
            [one] * len(group),
            [SMEM, SMEM, VMEM, VMEM],
            [VMEM] * len(group),
            flops=work * len(group),
            moved=read * len(group),
        )(table, deal, adjacency, pool_one)
        parts.update(zip(group, outs))
    parts = {(i, j): p if j == 0 else swap(p, "feat", j) for (i, j), p in parts.items()}
    columns = []
    for i in range(per):
        outs = call(
            functools.partial(dense_kernel, feats),
            [one] * feats,
            [VMEM] * (2 + feats),
            [VMEM] * feats,
            [pltpu.VMEM((size, weight_one.shape[1]), BF16)],
            flops=4 * size * weight_one.size,
            moved=weight_one.size * 4,
        )(weight_one, weight_two, *[parts[i, j] for j in range(feats)])
        columns += [c if j == 0 else swap(c, "feat", j) for j, c in enumerate(outs)]

    pair = call(
        second_pair_kernel,
        [block((2, size, width))],
        [VMEM] * feats,
        [VMEM],
        moved=8 * size * width,
    )(*columns[:feats])[0]
    own, *sends = call(
        functools.partial(second_kernel, domains, feats),
        [block((rows, size, width)), *near_far],
        [SMEM, SMEM] + [VMEM] * len(columns),
        [VMEM] * (1 + len(near_far)),
        moved=8 * size * width * domains,
    )(slots, deal, *columns)
    arrived = exchange(domains, own, pair, sends, which, "two")

    pool_two, leaving = call(
        functools.partial(leaving_sum_kernel, domains),
        [pool, block((2, size, width))],
        [SMEM, SMEM] + [VMEM] * (1 + len(arrived)),
        [VMEM] * 2,
        flops=work * 2,
        moved=read * 2,
        input_output_aliases={3: 0},
    )(table, slots, adjacency, *arrived)
    moved = lax.ppermute(leaving, "dom", [(i, (i + 1) % domains) for i in range(domains)])
    out = call(
        staying_sum_kernel,
        jax.ShapeDtypeStruct((rows, size, width), BF16),
        [SMEM, SMEM, VMEM, VMEM],
        VMEM,
        flops=work * (rows - 2),
        moved=read * (rows - 2),
    )(table, slots, adjacency, pool_two)
    out = call(
        place_kernel,
        jax.ShapeDtypeStruct((rows, size, width), BF16),
        [SMEM, VMEM, ANY],
        ANY,
        [pltpu.SemaphoreType.DMA((2,))],
        moved=4 * size * width * 2,
        input_output_aliases={2: 0},
    )(slots, moved, out)
    return out.reshape(rows * size, width)


def solution(mesh):
    in_specs = (P("dom", "feat"), P("dom", None, None, None), P(), P(), P(), P())
    return jax.shard_map(
        on_device, mesh=mesh, in_specs=in_specs, out_specs=P("dom", "feat"), check_vma=False
    )
```
